256 devices in a mesh: gx: 8 (over z), gy: 4 (over y), gz: 8 (over x, core).
Axes of the slice: x: 4, y: 4, z: 8, core: 2. Of those that a mesh axis runs over, the one named last changes fastest.
Arguments:
- fields: bfloat16 [65536, 2048], P(('gx', 'gy', 'gz')), may hold values from 0.5 to 1.5
- velocity: float32 [3, 128, 32, 1024], P(None, ('gx', 'gy'), 'gz'), may hold values from -3 to 3
- displacement: float32 [3, 128, 32, 1024], P(None, ('gx', 'gy'), 'gz'), may hold values from -2 to 2
- node_mass: float32 [128, 32, 1024], P(('gx', 'gy'), 'gz'), may hold values from 0.2 to 1
- remap_matrix: bfloat16 [2, 24576, 64, 64], P(None, ('gx', 'gy', 'gz')), may hold values from -1 to 4
- remap_source: int32 [2, 24576], P(None, ('gx', 'gy', 'gz')), may hold values from 0 to 255
- remap_target: int32 [2, 24576], P(None, ('gx', 'gy', 'gz')), may hold values from -1 to 255, as said below
Outputs:
- fields_out: bfloat16 [65536, 2048], P(('gx', 'gy', 'gz'))
- velocity_out: float32 [3, 128, 32, 1024], P(None, ('gx', 'gy'), 'gz')
- displacement_out: float32 [3, 128, 32, 1024], P(None, ('gx', 'gy'), 'gz')
The draws below stay inside these ranges and needn't reach their ends.
Inputs may be any that keep to these rules, and one draw needn't show every extreme that they name: `remap_target`: each device's slots form three blocks of 32 toward one lower, the same, one higher device along gx+gy; live slots come first in each block; the middle block is full; values are zones of the owner.
All inputs are finite; a program needn't handle non-finite values.
Results may differ from the reference program's by a relative error of at most 0.0063.
Values may be sent and summed in bfloat16 or wider, within the bound.
No kernel may reach another device: no remote copies, remote signals or barrier semaphores. Data moves between devices by JAX's collectives and lax.ppermute only.
A program may use at most 128 MiB of HBM per device.

```python
import math
import jax
import jax.numpy as jnp
import numpy as np
from jax import lax

NODES = 125
POINTS = 512
MODES = 64
FIELDS = 32
STEPS = 2
ZA = 1
ZB = 1
ZC = 256
CAP = 32
ZDEV = 256
SLOTS = 96
RANKS = 256
ZONES = 65536
NA = 128
NB = 32
NC = 1024
FIELD_WIDTH = 2048
N_GX = 8
N_GY = 4
N_GZ = 8


def draw_remap_matrix(key, part):
    first_key, second_key = jax.random.split(jax.random.fold_in(key, 11), 2)
    full_shape = (STEPS, RANKS * 3 * CAP, MODES, MODES)
    diagonal = jax.random.uniform(first_key, full_shape[:3], jnp.float32, 0.4, 1.0)
    spread = 0.06 * jnp.clip(jax.random.normal(second_key, full_shape, jnp.float32), -5.0, 5.0)
    matrices = spread + diagonal[..., None] * jnp.eye(MODES, dtype=jnp.float32)
    return matrices.astype(jnp.bfloat16)


def draw_remap_target(key, part):
    first_key, second_key = jax.random.split(jax.random.fold_in(key, 23), 2)
    counts = jax.random.randint(first_key, (STEPS, RANKS, 3), 0, CAP + 1, dtype=jnp.int32)
    counts = counts.at[:, :, 1].set(CAP)
    zones = jax.random.randint(second_key, (STEPS, RANKS, 3, CAP), 0, ZDEV, dtype=jnp.int32)
    position = jnp.arange(CAP, dtype=jnp.int32)
    live = position[None, None, None, :] < counts[..., None]
    chosen = jnp.where(live, zones, -1)
    return chosen.reshape(STEPS, RANKS * 3 * CAP).astype(jnp.int32)


def with_ends(values, own_key, smallest, largest):
    spot = [jax.random.randint(jax.random.fold_in(own_key, axis), (), 0, length) for axis, length in enumerate(values.shape)]
    longest = values.shape.index(max(values.shape))
    next_to = spot[:longest] + [(spot[longest] + 1) % values.shape[longest]] + spot[longest + 1:]
    return values.at[tuple(spot)].set(smallest).at[tuple(next_to)].set(largest)


def levels(key, extent, cuts, smallest, largest):
    def one(axis_at, shards_of):
        steps = jax.random.uniform(jax.random.fold_in(jax.random.fold_in(key, 6), axis_at), (shards_of,), jnp.float32, smallest / len(cuts), largest / len(cuts))
        return jnp.repeat(jnp.exp(steps), extent[axis_at] // shards_of).reshape((-1,) + (1,) * (len(extent) - axis_at - 1))

    factor_of = one(*cuts[0])
    for cut in cuts[1:]:
        factor_of = factor_of * one(*cut)
    return factor_of


def normal_values(rng, extent, width, bound, cuts=(), kind=jnp.bfloat16):
    drawn = width * jax.random.normal(rng, extent, jnp.float32)
    if cuts:
        drawn = drawn * levels(rng, extent, cuts, -0.22, 0.18)
    return jnp.clip(drawn, -bound, bound).astype(kind)


def setup_inputs(seed: int = 0) -> dict:
    key_of = jax.random.split(jax.random.key(seed), 8)
    return {
        "fields": jnp.clip(0.5 + 1.0 * jax.random.uniform(key_of[0], (ZONES, FIELD_WIDTH), jnp.float32) ** levels(key_of[0], (ZONES, FIELD_WIDTH), ((0, 256),), -0.2, 0.2), 0.5, 1.5).astype(jnp.bfloat16),
        "velocity": normal_values(key_of[1], (3, NA, NB, NC), 0.5, 3.0, ((1, 32), (2, 8)), jnp.float32),
        "displacement": normal_values(key_of[2], (3, NA, NB, NC), 0.3, 2.0, ((1, 32), (2, 8)), jnp.float32),
        "node_mass": jnp.clip(jnp.exp(math.log(1.0) - 1.609438 * jax.random.uniform(key_of[3], (NA, NB, NC), jnp.float32) ** levels(key_of[3], (NA, NB, NC), ((0, 32), (1, 8)), -0.2, 0.2)), 0.2, 1.0),
        "remap_matrix": draw_remap_matrix(jax.random.fold_in(key_of[7], 71), 0),
        "remap_source": with_ends(jax.random.randint(key_of[5], (STEPS, RANKS * SLOTS), 0, ZDEV), jax.random.fold_in(key_of[5], 1), 0, ZDEV - 1).astype(jnp.int32),
        "remap_target": draw_remap_target(jax.random.fold_in(key_of[7], 71), 0),
    }


TIME_STEP = 0.3
GAMMA_LESS = 0.4
VISCOSITY = 0.3
HIGHEST_PRECISION = lax.Precision.HIGHEST

def gauss_rule(order):
    if order == 8:
        half_points = [0.1834346424956498, 0.525532409916329, 0.7966664774136267, 0.9602898564975363]
        half_weights = [0.362683783378362, 0.3137066458778873, 0.2223810344533745, 0.1012285362903763]
    else:
        half_points = [0.3399810435848563, 0.8611363115940526]
        half_weights = [0.6521451548625461, 0.3478548451374538]
    points = np.array([-value for value in half_points[::-1]] + half_points)
    weights = np.array(half_weights[::-1] + half_weights)
    return (points, weights)

def lagrange_tables(nodes, points):
    values = np.ones((points.shape[0], nodes.shape[0]))
    slopes = np.zeros((points.shape[0], nodes.shape[0]))
    for column in range(nodes.shape[0]):
        for other in range(nodes.shape[0]):
            if other != column:
                values[:, column] *= (points - nodes[other]) / (nodes[column] - nodes[other])
        for other in range(nodes.shape[0]):
            if other != column:
                product = np.ones(points.shape) / (nodes[column] - nodes[other])
                for third in range(nodes.shape[0]):
                    if third != column and third != other:
                        product = product * (points - nodes[third]) / (nodes[column] - nodes[third])
                slopes[:, column] += product
    return (values, slopes)

def kron_three(first, second, third):
    return np.kron(np.kron(first, second), third)

def basis_tables():
    gauss_points, gauss_weights = gauss_rule(8)
    points = (gauss_points + 1.0) / 2.0
    weights = gauss_weights / 2.0
    root = math.sqrt(3.0 / 7.0)
    lobatto = (np.array([-1.0, -root, 0.0, root, 1.0]) + 1.0) / 2.0
    four_points, four_weights = gauss_rule(4)
    legendre_nodes = (four_points + 1.0) / 2.0
    node_values, node_slopes = lagrange_tables(lobatto, points)
    mode_values, unused_slopes = lagrange_tables(legendre_nodes, points)
    gradient_table = np.concatenate([kron_three(node_slopes, node_values, node_values), kron_three(node_values, node_slopes, node_values), kron_three(node_values, node_values, node_slopes)], 0)
    interpolate = kron_three(mode_values, mode_values, mode_values)
    weight_table = kron_three(weights, weights, weights)
    mass_diagonal = four_weights / 2.0
    project_line = mode_values.T * weights[None, :] / mass_diagonal[:, None]
    projection = kron_three(project_line, project_line, project_line)
    return (jnp.asarray(gradient_table.astype(np.float32), dtype=jnp.float32), jnp.asarray(interpolate.astype(np.float32), dtype=jnp.float32), jnp.asarray(weight_table.astype(np.float32), dtype=jnp.float32), jnp.asarray(projection.astype(np.float32), dtype=jnp.float32))

def split_zones(lattice, axis_index, count):
    leading = lax.slice_in_dim(lattice, 0, 4 * count, axis=axis_index)
    new_shape = lattice.shape[:axis_index] + (count, 4) + lattice.shape[axis_index + 1:]
    leading = leading.reshape(new_shape)
    trailing = lax.slice_in_dim(lattice, 4, 4 * count + 1, stride=4, axis=axis_index)
    trailing = jnp.expand_dims(trailing, axis_index + 1)
    return jnp.concatenate([leading, trailing], axis_index + 1)

def zone_nodes(extended):
    count_a = (extended.shape[1] - 1) // 4
    count_b = (extended.shape[2] - 1) // 4
    count_c = (extended.shape[3] - 1) // 4
    grid = split_zones(extended, 1, count_a)
    grid = split_zones(grid, 3, count_b)
    grid = split_zones(grid, 5, count_c)
    grid = jnp.transpose(grid, (0, 2, 4, 6, 1, 3, 5))
    return grid.reshape(3, NODES, count_a * count_b * count_c)

def join_zones(grid, axis_index):
    count = grid.shape[axis_index]
    leading = lax.slice_in_dim(grid, 0, 4, axis=axis_index + 1)
    leading = leading.reshape(grid.shape[:axis_index] + (4 * count,) + grid.shape[axis_index + 2:])
    trailing = lax.slice_in_dim(grid, 4, 5, axis=axis_index + 1)
    spacer = jnp.zeros_like(lax.slice_in_dim(trailing, 0, 1, axis=axis_index))
    trailing = jnp.concatenate([spacer, trailing], axis_index)
    filler = jnp.zeros_like(trailing)
    trailing = jnp.concatenate([trailing, filler, filler, filler], axis_index + 1)
    trailing = trailing.reshape(grid.shape[:axis_index] + (4 * count + 4,) + grid.shape[axis_index + 2:])
    trailing = lax.slice_in_dim(trailing, 0, 4 * count + 1, axis=axis_index)
    zero_end = jnp.zeros_like(lax.slice_in_dim(trailing, 0, 1, axis=axis_index))
    leading = jnp.concatenate([leading, zero_end], axis_index)
    return leading + trailing

def zone_forces(forces, count_a, count_b, count_c):
    grid = forces.reshape(3, 5, 5, 5, count_a, count_b, count_c)
    grid = jnp.transpose(grid, (0, 4, 1, 5, 2, 6, 3))
    grid = join_zones(grid, 5)
    grid = join_zones(grid, 3)
    return join_zones(grid, 1)

def fold_periodic(lattice, axis_index):
    length = lattice.shape[axis_index] - 1
    first = lax.slice_in_dim(lattice, 0, 1, axis=axis_index) + lax.slice_in_dim(lattice, length, length + 1, axis=axis_index)
    return jnp.concatenate([first, lax.slice_in_dim(lattice, 1, length, axis=axis_index)], axis_index)

def zone_kernel(zone_velocity, rho_modes, energy_modes, tables):
    gradient_table, interpolate, weight_table, projection = tables
    zones = zone_velocity.shape[2]
    flat_velocity = jnp.transpose(zone_velocity, (1, 0, 2)).reshape(NODES, 3 * zones)
    gradient = jnp.dot(gradient_table, flat_velocity, precision=HIGHEST_PRECISION).reshape(3, POINTS, 3, zones)
    point_values = jnp.dot(interpolate, jnp.concatenate([rho_modes, energy_modes], 1), precision=HIGHEST_PRECISION)
    rho_points = point_values[:, :zones]
    energy_points = point_values[:, zones:]
    divergence = gradient[0, :, 0] + gradient[1, :, 1] + gradient[2, :, 2]
    pressure = GAMMA_LESS * energy_points
    viscous = VISCOSITY * rho_points
    identity = jnp.eye(3, dtype=jnp.float32)
    stress = 0.5 * viscous[None, :, None, :] * (gradient + jnp.transpose(gradient, (2, 1, 0, 3)))
    stress = stress - identity[:, None, :, None] * pressure[None, :, None, :]
    heating = lax.optimization_barrier(jnp.sum(stress * gradient, axis=(0, 2)))
    weighted = stress * weight_table[None, :, None, None]
    forces = jnp.dot(gradient_table.T, weighted.reshape(3 * POINTS, 3 * zones), precision=HIGHEST_PRECISION)
    forces = jnp.transpose(forces.reshape(NODES, 3, zones), (1, 0, 2))
    rates = jnp.concatenate([-rho_points * divergence, heating - energy_points * divergence], 1)
    new_modes = jnp.concatenate([rho_modes, energy_modes], 1) + TIME_STEP * jnp.dot(projection, rates, precision=HIGHEST_PRECISION)
    return (forces, new_modes[:, :zones], new_modes[:, zones:])

def remap_fields(fields, matrices, source, target):
    blocks_a = N_GX * N_GY
    blocks_b = N_GZ
    ranks = blocks_a * blocks_b
    slots = 3 * CAP
    fields_ranked = fields.reshape(ranks, ZDEV, MODES * FIELDS)
    matrices_ranked = matrices.reshape(ranks, slots, MODES, MODES)
    source_ranked = source.reshape(ranks, slots)

    def contribute(pieces):
        rank_fields, rank_matrices, rank_source = pieces
        picked = jnp.take(rank_fields, rank_source, axis=0).reshape(slots, MODES, FIELDS)
        result = jnp.einsum('pij,pjf->pif', rank_matrices.astype(jnp.float32), picked.astype(jnp.float32), precision=HIGHEST_PRECISION)
        return result.astype(jnp.bfloat16).reshape(slots, MODES * FIELDS)
    contributions = lax.map(contribute, (fields_ranked, matrices_ranked, source_ranked))
    rank_ids = jnp.arange(ranks, dtype=jnp.int32)
    rank_first = rank_ids // blocks_b
    rank_second = rank_ids % blocks_b
    direction = jnp.arange(3, dtype=jnp.int32) - 1
    owner = (rank_first[:, None] + direction[None, :]) % blocks_a * blocks_b + rank_second[:, None]
    owner = jnp.repeat(owner, CAP, axis=1)
    target_ranked = target.reshape(ranks, slots)
    global_index = jnp.where(target_ranked >= 0, owner * ZDEV + target_ranked, ranks * ZDEV).astype(jnp.int32)
    summed = jnp.zeros((ranks * ZDEV, MODES * FIELDS), jnp.float32)
    summed = summed.at[global_index.reshape(-1)].add(contributions.reshape(-1, MODES * FIELDS).astype(jnp.float32), mode='drop')
    return summed.astype(jnp.bfloat16)

def reference(fields, velocity, displacement, node_mass, remap_matrix, remap_source, remap_target):
    tables = basis_tables()
    blocks_a = N_GX * N_GY
    blocks_b = N_GZ
    zones_a = ZA * blocks_a
    zones_b = ZB * blocks_b
    total = ZONES
    blocks = total // ZDEV
    for step in range(STEPS):
        extended = jnp.concatenate([velocity, velocity[:, :1]], 1)
        extended = jnp.concatenate([extended, extended[:, :, :1]], 2)
        extended = jnp.concatenate([extended, extended[:, :, :, :1]], 3)
        zone_velocity = zone_nodes(extended)
        spatial = fields.reshape(blocks_a, blocks_b, ZA, ZB, ZC, MODES * FIELDS)
        spatial = jnp.transpose(spatial, (0, 2, 1, 3, 4, 5)).reshape(total, MODES, FIELDS)
        rho_modes = spatial[:, :, 0].T.astype(jnp.float32)
        energy_modes = spatial[:, :, 1].T.astype(jnp.float32)
        velocity_blocks = jnp.transpose(zone_velocity.reshape(3, NODES, blocks, ZDEV), (2, 0, 1, 3))
        rho_blocks = jnp.transpose(rho_modes.reshape(MODES, blocks, ZDEV), (1, 0, 2))
        energy_blocks = jnp.transpose(energy_modes.reshape(MODES, blocks, ZDEV), (1, 0, 2))

        def one_block(pieces):
            return zone_kernel(pieces[0], pieces[1], pieces[2], tables)
        forces, rho_new, energy_new = lax.map(one_block, (velocity_blocks, rho_blocks, energy_blocks))
        forces = jnp.transpose(forces, (1, 2, 0, 3)).reshape(3, NODES, total)
        rho_new = jnp.transpose(rho_new, (1, 0, 2)).reshape(MODES, total)
        energy_new = jnp.transpose(energy_new, (1, 0, 2)).reshape(MODES, total)
        nodal = zone_forces(forces, zones_a, zones_b, ZC)
        nodal = fold_periodic(nodal, 3)
        nodal = fold_periodic(nodal, 2)
        nodal = fold_periodic(nodal, 1)
        velocity = velocity - TIME_STEP * nodal / node_mass[None]
        displacement = displacement + TIME_STEP * velocity
        updated = jnp.concatenate([rho_new.T[:, :, None].astype(jnp.bfloat16), energy_new.T[:, :, None].astype(jnp.bfloat16), spatial[:, :, 2:]], 2)
        updated = updated.reshape(blocks_a, ZA, blocks_b, ZB, ZC, MODES * FIELDS)
        updated = jnp.transpose(updated, (0, 2, 1, 3, 4, 5)).reshape(total, MODES * FIELDS)
        fields = remap_fields(updated, remap_matrix[step], remap_source[step], remap_target[step])
    return (fields, velocity, displacement)
```

```python
import math

import jax
import jax.numpy as jnp
import numpy as np
from jax import lax
from jax.experimental import pallas as pl
from jax.experimental.pallas import tpu as pltpu
from jax.sharding import PartitionSpec as P

NODES = 125
POINTS = 512
MODES = 64
FIELDS = 32
STEPS = 2


TIME_STEP = 0.3
GAMMA_LESS = 0.4
VISCOSITY = 0.3
F32 = jnp.float32
BF16 = jnp.bfloat16
ZONE_COUNT = 256
ROWS = 32
LINE = 1024
CAPACITY = 32
SLOTS = 96
WIDTH = MODES * FIELDS
SENT = WIDTH + 128


def from_behind(shard, axis, by):
    size = lax.axis_size(axis)
    return lax.ppermute(shard, axis, [(i, (i + by) % size) for i in range(size)])


def gauss_rule(order):
    if order == 8:
        half_points = [
            0.1834346424956498,
            0.525532409916329,
            0.7966664774136267,
            0.9602898564975363,
        ]
        half_weights = [
            0.362683783378362,
            0.3137066458778873,
            0.2223810344533745,
            0.1012285362903763,
        ]
    else:
        half_points = [0.3399810435848563, 0.8611363115940526]
        half_weights = [0.6521451548625461, 0.3478548451374538]
    points = np.array([-value for value in half_points[::-1]] + half_points)
    weights = np.array(half_weights[::-1] + half_weights)
    return (points, weights)


def lagrange_tables(nodes, points):
    values = np.ones((points.shape[0], nodes.shape[0]))
    slopes = np.zeros((points.shape[0], nodes.shape[0]))
    for column in range(nodes.shape[0]):
        for other in range(nodes.shape[0]):
            if other != column:
                values[:, column] *= (points - nodes[other]) / (nodes[column] - nodes[other])
        for other in range(nodes.shape[0]):
            if other != column:
                product = np.ones(points.shape) / (nodes[column] - nodes[other])
                for third in range(nodes.shape[0]):
                    if third != column and third != other:
                        product = product * (points - nodes[third]) / (nodes[column] - nodes[third])
                slopes[:, column] += product
    return (values, slopes)


def kron_three(first, second, third):
    return np.kron(np.kron(first, second), third)


def split_table(table):
    high = table.astype(jnp.bfloat16)
    low = (table - high.astype(np.float32)).astype(jnp.bfloat16)
    return (high, low)


def node_columns(table):
    grid = table.reshape(-1, 5, 25 // 5, 5).transpose(0, 3, 1, 2).reshape(-1, 5, 25)
    return np.pad(grid, ((0, 0), (0, 0), (0, ROWS - 25))).reshape(-1, 5 * ROWS)


def basis_tables():
    gauss_points, gauss_weights = gauss_rule(8)
    points = (gauss_points + 1.0) / 2.0
    weights = gauss_weights / 2.0
    root = math.sqrt(3.0 / 7.0)
    lobatto = (np.array([-1.0, -root, 0.0, root, 1.0]) + 1.0) / 2.0
    four_points, four_weights = gauss_rule(4)
    legendre_nodes = (four_points + 1.0) / 2.0
    node_values, node_slopes = lagrange_tables(lobatto, points)
    mode_values, unused_slopes = lagrange_tables(legendre_nodes, points)
    gradient_table = np.concatenate(
        [
            kron_three(node_slopes, node_values, node_values),
            kron_three(node_values, node_slopes, node_values),
            kron_three(node_values, node_values, node_slopes),
        ],
        0,
    )
    interpolate = kron_three(mode_values, mode_values, mode_values)
    weight_table = kron_three(weights, weights, weights)
    mass_diagonal = four_weights / 2.0
    project_line = mode_values.T * weights[None, :] / mass_diagonal[:, None]
    projection = kron_three(project_line, project_line, project_line)
    gradient_table = gradient_table.astype(np.float32)
    weighted_table = gradient_table * np.tile(weight_table.astype(np.float32), 3)[:, None]
    grad_hi, grad_lo = split_table(node_columns(gradient_table))
    force_hi, force_lo = split_table(node_columns(weighted_table).T)
    inter_hi, inter_lo = split_table(interpolate.astype(np.float32))
    proj_hi, proj_lo = split_table(projection.astype(np.float32))
    return (
        jnp.asarray(np.concatenate([grad_hi, grad_hi, grad_lo], 1)),
        jnp.asarray(np.concatenate([force_hi, force_lo], 0)),
        jnp.asarray(np.concatenate([inter_hi, inter_lo], 1)),
        jnp.asarray(np.concatenate([proj_hi, proj_lo], 0)),
    )


def split_two(values):
    high = values.astype(BF16)
    return (high, (values - high.astype(F32)).astype(BF16))


def split_three(values):
    high = values.astype(BF16)
    rest = values - high.astype(F32)
    middle = rest.astype(BF16)
    return (high, middle, (rest - middle.astype(F32)).astype(BF16))


def mm(left, right, dims=((1,), (0,))):
    return lax.dot_general(left, right, (dims, ((), ())), preferred_element_type=F32)


def iota(shape, axis):
    return lax.broadcasted_iota(jnp.int32, shape, axis)


def line_selector(to_zones):
    lattice = iota((512, 512), 0 if to_zones else 1)
    grouped = iota((512, 512), 1 if to_zones else 0)
    return jnp.where(4 * (grouped % 128) + grouped // 128 == lattice, 1.0, 0.0).astype(BF16)


def mode_columns():
    row = iota((2 * MODES, WIDTH), 0)
    column = iota((2 * MODES, WIDTH), 1)
    return jnp.where(FIELDS * (row % MODES) + row // MODES == column, 1.0, 0.0).astype(BF16)


def pick_modes(fields):
    return mm(mode_columns(), fields, ((1,), (1,)))


def zone_math(velocity_of, modes, grad_ref, force_ref, inter_ref, proj_ref, nodes_ref, high_ref, low_ref,
              rate_high_ref, rate_low_ref, lattice_ref, face_up_ref, face_down_ref, modes_ref):
    zones = ZONE_COUNT
    for comp in range(3):
        line = velocity_of(comp)
        lanes = slice(zones * comp, zones * (comp + 1))
        groups = [line[:, zones * u : zones * (u + 1)] for u in range(4)]
        groups.append(pltpu.roll(groups[0], zones - 1, 1))
        for u in range(5):
            high, low = split_two(groups[u])
            nodes_ref[ROWS * u : ROWS * (u + 1), lanes] = high
            nodes_ref[ROWS * (5 + u) : ROWS * (6 + u), lanes] = low
            nodes_ref[ROWS * (10 + u) : ROWS * (11 + u), lanes] = high
    both = jnp.concatenate([modes[:MODES], modes[MODES:]], 1)
    twice = jnp.concatenate([both, both], 0).astype(BF16)
    chunk = 128
    for part in range(POINTS // chunk):
        rows = slice(chunk * part, chunk * (part + 1))
        nodes = nodes_ref[...]
        grads = []
        for first in range(3):
            start = POINTS * first + chunk * part
            flat = mm(grad_ref[start : start + chunk, :], nodes)
            grads.append([flat[:, zones * c : zones * (c + 1)] for c in range(3)])
        points = mm(inter_ref[rows, :], twice)
        rho = points[:, :zones]
        energy = points[:, zones:]
        divergence = grads[0][0] + grads[1][1] + grads[2][2]
        pressure = GAMMA_LESS * energy
        viscous = 0.5 * VISCOSITY * rho
        heating = None
        for first in range(3):
            for second in range(first, 3):
                total = grads[first][second] + grads[second][first]
                entry = viscous * total
                if first == second:
                    entry = entry - pressure
                    work = entry * grads[first][first]
                else:
                    work = entry * total
                heating = work if heating is None else heating + work
                high, low = split_two(entry)
                for d, c in ((first, second), (second, first))[: 1 if first == second else 2]:
                    at = slice(POINTS * d + chunk * part, POINTS * d + chunk * (part + 1))
                    lanes = slice(zones * c, zones * (c + 1))
                    high_ref[at, lanes] = high
                    low_ref[at, lanes] = low
        for column, rate in ((0, -rho * divergence), (zones, heating - energy * divergence)):
            high, low = split_two(rate)
            rate_high_ref[rows, column : column + zones] = high
            rate_low_ref[rows, column : column + zones] = low
    nodal = 5 * ROWS
    main = mm(force_ref[...], high_ref[...])
    force = main[:nodal] + main[nodal:] + mm(force_ref[:nodal, :], low_ref[...])
    for comp in range(3):
        lanes = slice(zones * comp, zones * (comp + 1))
        for u in range(4):
            block = force[ROWS * u : ROWS * (u + 1), lanes]
            if u == 0:
                block = block + pltpu.roll(force[ROWS * 4 : ROWS * 5, lanes], 1, 1)
            lattice_ref[comp, :, zones * u : zones * (u + 1)] = block
    for comp in range(3):
        for s in range(5):
            face_up_ref[5 * comp + s, :] = lattice_ref[comp, 5 * s + 4, :]
            if face_down_ref is not None:
                face_down_ref[5 * comp + s, :] = lattice_ref[comp, 5 * s, :]
    main = mm(proj_ref[...], rate_high_ref[...])
    change = main[:MODES] + main[MODES:] + mm(proj_ref[:MODES, :], rate_low_ref[...])
    both = both + TIME_STEP * change
    modes_ref[:MODES, :] = both[:, :zones].astype(BF16)
    modes_ref[MODES:, :] = both[:, zones:].astype(BF16)


def zone_first_kernel(velocity_ref, mass_ref, halo_a_ref, halo_b_ref, halo_c_ref, fields_ref, grad_ref, force_ref,
                      inter_ref, proj_ref, state_ref, lattice_ref, up_ref, down_ref, modes_ref,
                      native_ref, *scratch):
    for comp in range(4):
        base = ROWS * comp
        native_ref[base + 24 : base + 32, :] = jnp.full((8, LINE), 1.0 if comp == 3 else 0.0, F32)
        for s in range(4):
            own = mass_ref[s] if comp == 3 else velocity_ref[comp, s]
            native_ref[base + 5 * s : base + 5 * s + 4, :] = own
            native_ref[base + 5 * s + 4, :] = halo_b_ref[comp, s, :]
        native_ref[base + 20 : base + 24, :] = halo_a_ref[comp]
        native_ref[base + 24, :] = halo_c_ref[comp, 0, :]
    selector = line_selector(True)
    count = 4 * ROWS
    for half in range(2):
        pieces = jnp.concatenate(split_three(native_ref[:, 512 * half : 512 * (half + 1)]), 0)
        moved = mm(pieces, selector)
        moved = moved[:count] + moved[count : 2 * count] + moved[2 * count :]
        for comp in range(4):
            for u in range(4):
                lanes = slice(256 * u + 128 * half, 256 * u + 128 * (half + 1))
                state_ref[comp, :, lanes] = moved[ROWS * comp : ROWS * (comp + 1), 128 * u : 128 * (u + 1)]
    modes = pick_modes(fields_ref[...])
    zone_math(lambda comp: state_ref[comp], modes, grad_ref, force_ref, inter_ref, proj_ref, *scratch,
              lattice_ref, up_ref, down_ref, modes_ref)


def zone_second_kernel(state_ref, first_ref, low_ref, upper_ref, block_0_ref, block_1_ref, block_2_ref, grad_ref,
                       force_ref, inter_ref, proj_ref, fields_ref, total_ref, lattice_ref, up_ref, modes_ref,
                       *scratch):
    fields = sum_slots(block_0_ref, block_1_ref, block_2_ref)
    fields_ref[...] = fields
    total_ref[...] = first_ref[...]
    for comp in range(3):
        total_ref[comp, 0:5, :] = total_ref[comp, 0:5, :] + low_ref[5 * comp : 5 * comp + 5, :]
        total_ref[comp, 20:25, :] = total_ref[comp, 20:25, :] + upper_ref[5 * comp : 5 * comp + 5, :]
    factor = TIME_STEP / state_ref[3]
    modes = pick_modes(fields)
    zone_math(lambda comp: state_ref[comp] - total_ref[comp] * factor, modes, grad_ref, force_ref, inter_ref,
              proj_ref, *scratch, lattice_ref, up_ref, None, modes_ref)


def sum_slots(*block_refs):
    incoming = jnp.concatenate([ref[...] for ref in block_refs], 0)
    codes = incoming[:, WIDTH:].astype(F32)
    label = iota((SLOTS, 128), 1).astype(F32)
    chosen = [jnp.where(codes == label + 128.0 * half, 1.0, 0.0).astype(BF16) for half in range(ZONE_COUNT // 128)]
    selector = jnp.concatenate(chosen, 1)
    return mm(selector, incoming[:, :WIDTH], ((0,), (0,))).astype(BF16)


def sum_kernel(block_0_ref, block_1_ref, block_2_ref, out_ref):
    out_ref[...] = sum_slots(block_0_ref, block_1_ref, block_2_ref)


def remap_kernel(step, fields_ref, modes_ref, matrix_ref, source_ref, target_ref, low_ref, middle_ref, upper_ref,
                 picked_ref, result_ref):
    zone = iota((ZONE_COUNT, SLOTS), 0)
    chosen = jnp.where(zone == source_ref[step : step + 1, :], 1.0, 0.0).astype(BF16)
    picked = mm(chosen, fields_ref[...], ((0,), (0,)))
    new = mm(chosen, modes_ref[...].T, ((0,), (0,))).astype(BF16)
    new = mm(new, mode_columns())
    lane = iota((SLOTS, 128), 1)
    group = lane // FIELDS
    renewed = lane % FIELDS < 2
    for g in range(WIDTH // 128):
        lanes = slice(128 * g, 128 * (g + 1))
        piece = jnp.where(renewed, new[:, lanes], picked[:, lanes])
        for r in range(4):
            picked_ref[pl.ds(4 * g + r, SLOTS, stride=MODES), :] = jnp.where(group == r, piece, 0.0)

    def multiply(trip, carry):
        for inner in range(8):
            slot = 8 * trip + inner
            at = pl.ds(pl.multiple_of(MODES * slot, MODES), MODES)
            result_ref[at, :] = mm(matrix_ref[0, slot], picked_ref[at, :].astype(BF16))
        return carry

    lax.fori_loop(0, SLOTS // 8, multiply, 0)
    outs = (low_ref, middle_ref, upper_ref)
    for g in range(WIDTH // 128):
        rows = [result_ref[pl.ds(4 * g + r, SLOTS, stride=MODES), :] for r in range(4)]
        total = None
        for shift in range(4):
            mixed = rows[3]
            for r in range(3):
                mixed = jnp.where(group == (r + shift) % 4, rows[r], mixed)
            if shift:
                mixed = pltpu.roll(mixed, 128 - FIELDS * shift, 1)
            total = mixed if total is None else total + mixed
        total = total.astype(BF16)
        for block in range(3):
            outs[block][:, 128 * g : 128 * (g + 1)] = total[CAPACITY * block : CAPACITY * (block + 1)]
    codes = jnp.broadcast_to(target_ref[step : step + 1, :].astype(F32), (8, SLOTS))
    codes = jnp.where(iota((8, SLOTS), 0) == 0, codes, 0.0).astype(BF16)
    codes = mm(codes, jnp.ones((8, 128), BF16), ((0,), (0,))).astype(BF16)
    for block in range(3):
        outs[block][:, WIDTH:] = codes[CAPACITY * block : CAPACITY * (block + 1)]


def fold_kernel(both, lattice_ref, *refs):
    if both:
        low_ref, upper_ref, out_ref, face_up_ref, face_down_ref = refs
    else:
        low_ref, out_ref, face_up_ref = refs
    out_ref[...] = lattice_ref[...]
    for comp in range(3):
        for s in range(5):
            out_ref[comp, 5 * s, :] = out_ref[comp, 5 * s, :] + low_ref[5 * comp + s, :]
            if both:
                out_ref[comp, 5 * s + 4, :] = out_ref[comp, 5 * s + 4, :] + upper_ref[5 * comp + s, :]
    for comp in range(3):
        face_up_ref[5 * comp : 5 * comp + 5, :] = out_ref[comp, 20:25, :]
        if both:
            face_down_ref[5 * comp : 5 * comp + 5, :] = out_ref[comp, 0:5, :]


def final_kernel(velocity_ref, displacement_ref, mass_ref, first_ref, second_ref, low_ref, velocity_out_ref,
                 displacement_out_ref, stage_ref, force_ref):
    for comp in range(3):
        for s in range(4):
            at = 16 * comp + 4 * s
            stage_ref[at : at + 4, :] = first_ref[comp, 5 * s : 5 * s + 4, :]
            second = second_ref[comp, 5 * s : 5 * s + 4, :]
            if s == 0:
                second = second + low_ref[5 * comp : 5 * comp + 4, :]
            stage_ref[48 + at : 48 + at + 4, :] = second
    selector = line_selector(False)
    for half in range(2):
        grouped = jnp.concatenate(
            [stage_ref[:, 256 * u + 128 * half : 256 * u + 128 * (half + 1)] for u in range(4)], 1
        )
        moved = mm(jnp.concatenate(split_two(grouped), 0), selector)
        force_ref[:, 512 * half : 512 * (half + 1)] = moved[:96] + moved[96:]
    for s in range(4):
        factor = TIME_STEP / mass_ref[s]
        for comp in range(3):
            at = 16 * comp + 4 * s
            middle = velocity_ref[comp, s] - force_ref[at : at + 4, :] * factor
            last = middle - force_ref[48 + at : 48 + at + 4, :] * factor
            velocity_out_ref[comp, s] = last
            displacement_out_ref[comp, s] = displacement_ref[comp, s] + TIME_STEP * middle + TIME_STEP * last


def shape(*dims, dtype=F32):
    return jax.ShapeDtypeStruct(dims, dtype)


LATTICE = (3, ROWS, LINE)
FACE = (15, LINE)


def zone_scratch():
    return [
        pltpu.VMEM((15 * ROWS, 3 * ZONE_COUNT), BF16),
        pltpu.VMEM((3 * POINTS, 3 * ZONE_COUNT), BF16),
        pltpu.VMEM((3 * POINTS, 3 * ZONE_COUNT), BF16),
        pltpu.VMEM((POINTS, 2 * ZONE_COUNT), BF16),
        pltpu.VMEM((POINTS, 2 * ZONE_COUNT), BF16),
    ]


def remap_call(step, fields, modes, matrix, source, target):
    whole = lambda *dims: pl.BlockSpec(dims, lambda i: (0,) * len(dims))
    block = shape(CAPACITY, SENT, dtype=BF16)
    return pl.pallas_call(
        lambda *refs: remap_kernel(step, *refs),
        grid=(1,),
        in_specs=[
            whole(ZONE_COUNT, WIDTH),
            whole(2 * MODES, ZONE_COUNT),
            pl.BlockSpec((1, SLOTS, MODES, MODES), lambda i: (step, 0, 0, 0)),
            whole(STEPS, SLOTS),
            whole(STEPS, SLOTS),
        ],
        out_specs=[whole(CAPACITY, SENT)] * 3,
        out_shape=[block] * 3,
        scratch_shapes=[pltpu.VMEM((SLOTS * MODES, 128), F32)] * 2,
        name="remap_step",
    )(fields, modes, matrix, source, target)


def body(fields, velocity, displacement, node_mass, remap_matrix, remap_source, remap_target):
    tables = basis_tables()
    lines = ("gx", "gy")
    send_a = jnp.concatenate([velocity[:, 0], node_mass[None, 0]], 0)
    send_b = jnp.concatenate([velocity[:, :, 0], node_mass[None, :, 0]], 0)
    send_c = send_a[:, :1]
    size_a = lax.axis_size(lines)
    size_b = lax.axis_size("gz")
    corner = [
        (((i + 1) % size_a) * size_b + (j + 1) % size_b, i * size_b + j)
        for i in range(size_a)
        for j in range(size_b)
    ]
    halo_a = from_behind(send_a, lines, -1)
    halo_b = from_behind(send_b, "gz", -1)
    halo_c = lax.ppermute(send_c, ("gx", "gy", "gz"), corner)
    lattice = shape(*LATTICE)
    face = shape(*FACE)
    modes_shape = shape(2 * MODES, ZONE_COUNT, dtype=BF16)
    state, partial, up, down, modes = pl.pallas_call(
        zone_first_kernel,
        out_shape=[shape(4, ROWS, LINE), lattice, face, face, modes_shape],
        scratch_shapes=[pltpu.VMEM((4 * ROWS, LINE), F32)] + zone_scratch(),
        name="zone_first",
    )(velocity, node_mass, halo_a, halo_b, halo_c, fields, *tables)
    from_low = from_behind(up, "gz", 1)
    from_up = from_behind(down, "gz", -1)
    low, middle, upper = remap_call(0, fields, modes, remap_matrix, remap_source, remap_target)
    in_upper = from_behind(upper, lines, 1)
    in_low = from_behind(low, lines, -1)
    partial, up, down = pl.pallas_call(
        lambda *refs: fold_kernel(True, *refs), out_shape=[lattice, face, face], name="fold_first"
    )(partial, from_low, from_up)
    from_low = from_behind(up, lines, 1)
    from_up = from_behind(down, lines, -1)
    fields, first, partial, up, modes = pl.pallas_call(
        zone_second_kernel,
        out_shape=[shape(ZONE_COUNT, WIDTH, dtype=BF16), lattice, lattice, face, modes_shape],
        scratch_shapes=zone_scratch(),
        name="zone_second",
    )(state, partial, from_low, from_up, middle, in_upper, in_low, *tables)
    from_low = from_behind(up, "gz", 1)
    low, middle, upper = remap_call(1, fields, modes, remap_matrix, remap_source, remap_target)
    in_upper = from_behind(upper, lines, 1)
    in_low = from_behind(low, lines, -1)
    partial, up = pl.pallas_call(
        lambda *refs: fold_kernel(False, *refs), out_shape=[lattice, face], name="fold_second"
    )(partial, from_low)
    from_low = from_behind(up, lines, 1)
    velocity_out, displacement_out = pl.pallas_call(
        final_kernel,
        out_shape=[shape(*velocity.shape), shape(*velocity.shape)],
        scratch_shapes=[pltpu.VMEM((96, LINE), F32)] * 2,
        name="final_update",
    )(velocity, displacement, node_mass, first, partial, from_low)
    fields_out = pl.pallas_call(
        sum_kernel, out_shape=shape(ZONE_COUNT, WIDTH, dtype=BF16), name="final_sum"
    )(middle, in_upper, in_low)
    return (fields_out, velocity_out, displacement_out)


def solution(mesh):
    in_specs = (
        P(("gx", "gy", "gz"), None),
        P(None, ("gx", "gy"), "gz", None),
        P(None, ("gx", "gy"), "gz", None),
        P(("gx", "gy"), "gz", None),
        P(None, ("gx", "gy", "gz"), None, None),
        P(None, ("gx", "gy", "gz")),
        P(None, ("gx", "gy", "gz")),
    )
    out_specs = (
        P(("gx", "gy", "gz"), None),
        P(None, ("gx", "gy"), "gz", None),
        P(None, ("gx", "gy"), "gz", None),
    )
    return jax.shard_map(body, mesh=mesh, in_specs=in_specs, out_specs=out_specs, check_vma=False)
```

```python
import math

import jax
import jax.numpy as jnp
import numpy as np
from jax import lax
from jax.experimental import pallas as pl
from jax.experimental.pallas import tpu as pltpu
from jax.sharding import PartitionSpec as P

NODES = 125
POINTS = 512
MODES = 64
FIELDS = 32
STEPS = 2


TIME_STEP = 0.3
GAMMA_LESS = 0.4
VISCOSITY = 0.3
F32 = jnp.float32
BF16 = jnp.bfloat16
ZONE_COUNT = 256
ROWS = 32
LINE = 1024
CAPACITY = 32
SLOTS = 96
WIDTH = MODES * FIELDS
SENT = WIDTH + 128
FOLDED = CAPACITY + 16


def from_behind(shard, axis, by):
    size = lax.axis_size(axis)
    return lax.ppermute(shard, axis, [(i, (i + by) % size) for i in range(size)])


def gauss_rule(order):
    if order == 8:
        half_points = [
            0.1834346424956498,
            0.525532409916329,
            0.7966664774136267,
            0.9602898564975363,
        ]
        half_weights = [
            0.362683783378362,
            0.3137066458778873,
            0.2223810344533745,
            0.1012285362903763,
        ]
    else:
        half_points = [0.3399810435848563, 0.8611363115940526]
        half_weights = [0.6521451548625461, 0.3478548451374538]
    points = np.array([-value for value in half_points[::-1]] + half_points)
    weights = np.array(half_weights[::-1] + half_weights)
    return (points, weights)


def lagrange_tables(nodes, points):
    values = np.ones((points.shape[0], nodes.shape[0]))
    slopes = np.zeros((points.shape[0], nodes.shape[0]))
    for column in range(nodes.shape[0]):
        for other in range(nodes.shape[0]):
            if other != column:
                values[:, column] *= (points - nodes[other]) / (nodes[column] - nodes[other])
        for other in range(nodes.shape[0]):
            if other != column:
                product = np.ones(points.shape) / (nodes[column] - nodes[other])
                for third in range(nodes.shape[0]):
                    if third != column and third != other:
                        product = product * (points - nodes[third]) / (nodes[column] - nodes[third])
                slopes[:, column] += product
    return (values, slopes)


def kron_three(first, second, third):
    return np.kron(np.kron(first, second), third)


def split_table(table):
    high = table.astype(jnp.bfloat16)
    low = (table - high.astype(np.float32)).astype(jnp.bfloat16)
    return (high, low)


def node_columns(table):
    grid = table.reshape(-1, 5, 25 // 5, 5).transpose(0, 3, 1, 2).reshape(-1, 5, 25)
    return np.pad(grid, ((0, 0), (0, 0), (0, ROWS - 25))).reshape(-1, 5 * ROWS)


def basis_tables():
    gauss_points, gauss_weights = gauss_rule(8)
    points = (gauss_points + 1.0) / 2.0
    weights = gauss_weights / 2.0
    root = math.sqrt(3.0 / 7.0)
    lobatto = (np.array([-1.0, -root, 0.0, root, 1.0]) + 1.0) / 2.0
    four_points, four_weights = gauss_rule(4)
    legendre_nodes = (four_points + 1.0) / 2.0
    node_values, node_slopes = lagrange_tables(lobatto, points)
    mode_values, unused_slopes = lagrange_tables(legendre_nodes, points)
    gradient_table = np.concatenate(
        [
            kron_three(node_slopes, node_values, node_values),
            kron_three(node_values, node_slopes, node_values),
            kron_three(node_values, node_values, node_slopes),
        ],
        0,
    )
    interpolate = kron_three(mode_values, mode_values, mode_values)
    weight_table = kron_three(weights, weights, weights)
    mass_diagonal = four_weights / 2.0
    project_line = mode_values.T * weights[None, :] / mass_diagonal[:, None]
    projection = kron_three(project_line, project_line, project_line)
    gradient_table = gradient_table.astype(np.float32)
    weighted_table = gradient_table * np.tile(weight_table.astype(np.float32), 3)[:, None]
    grad_hi, grad_lo = split_table(node_columns(gradient_table))
    force_hi, force_lo = split_table(node_columns(weighted_table).T)
    inter_hi, inter_lo = split_table(interpolate.astype(np.float32))
    proj_hi, proj_lo = split_table(projection.astype(np.float32))
    return (
        jnp.asarray(np.concatenate([grad_hi, grad_hi, grad_lo], 1)),
        jnp.asarray(np.concatenate([force_hi, force_lo], 0)),
        jnp.asarray(np.concatenate([inter_hi, inter_lo], 1)),
        jnp.asarray(np.concatenate([proj_hi, proj_lo], 0)),
    )


def split_two(values):
    high = values.astype(BF16)
    return (high, (values - high.astype(F32)).astype(BF16))


def split_three(values):
    high = values.astype(BF16)
    rest = values - high.astype(F32)
    middle = rest.astype(BF16)
    return (high, middle, (rest - middle.astype(F32)).astype(BF16))


def mm(left, right, dims=((1,), (0,))):
    return lax.dot_general(left, right, (dims, ((), ())), preferred_element_type=F32)


def iota(shape, axis):
    return lax.broadcasted_iota(jnp.int32, shape, axis)


def line_selector(to_zones):
    lattice = iota((512, 512), 0 if to_zones else 1)
    grouped = iota((512, 512), 1 if to_zones else 0)
    return jnp.where(4 * (grouped % 128) + grouped // 128 == lattice, 1.0, 0.0).astype(BF16)


def mode_columns():
    row = iota((2 * MODES, WIDTH), 0)
    column = iota((2 * MODES, WIDTH), 1)
    return jnp.where(FIELDS * (row % MODES) + row // MODES == column, 1.0, 0.0).astype(BF16)


def pick_modes(fields):
    return mm(mode_columns(), fields, ((1,), (1,)))


def zone_math(velocity_of, modes, grad_ref, force_ref, inter_ref, proj_ref, nodes_ref, high_ref, low_ref,
              rate_high_ref, rate_low_ref, lattice_ref, face_up_ref, edge_up_ref, face_down_ref, edge_down_ref, modes_ref):
    zones = ZONE_COUNT
    for comp in range(3):
        line = velocity_of(comp)
        lanes = slice(zones * comp, zones * (comp + 1))
        groups = [line[:, zones * u : zones * (u + 1)] for u in range(4)]
        groups.append(pltpu.roll(groups[0], zones - 1, 1))
        for u in range(5):
            high, low = split_two(groups[u])
            nodes_ref[ROWS * u : ROWS * (u + 1), lanes] = high
            nodes_ref[ROWS * (5 + u) : ROWS * (6 + u), lanes] = low
            nodes_ref[ROWS * (10 + u) : ROWS * (11 + u), lanes] = high
    both = jnp.concatenate([modes[:MODES], modes[MODES:]], 1)
    twice = jnp.concatenate([both, both], 0).astype(BF16)
    chunk = 128
    for part in range(POINTS // chunk):
        rows = slice(chunk * part, chunk * (part + 1))
        nodes = nodes_ref[...]
        grads = []
        for first in range(3):
            start = POINTS * first + chunk * part
            flat = mm(grad_ref[start : start + chunk, :], nodes)
            grads.append([flat[:, zones * c : zones * (c + 1)] for c in range(3)])
        points = mm(inter_ref[rows, :], twice)
        rho = points[:, :zones]
        energy = points[:, zones:]
        divergence = grads[0][0] + grads[1][1] + grads[2][2]
        pressure = GAMMA_LESS * energy
        viscous = 0.5 * VISCOSITY * rho
        heating = None
        for first in range(3):
            for second in range(first, 3):
                total = grads[first][second] + grads[second][first]
                entry = viscous * total
                if first == second:
                    entry = entry - pressure
                    work = entry * grads[first][first]
                else:
                    work = entry * total
                heating = work if heating is None else heating + work
                high, low = split_two(entry)
                for d, c in ((first, second), (second, first))[: 1 if first == second else 2]:
                    at = slice(POINTS * d + chunk * part, POINTS * d + chunk * (part + 1))
                    lanes = slice(zones * c, zones * (c + 1))
                    high_ref[at, lanes] = high
                    low_ref[at, lanes] = low
        for column, rate in ((0, -rho * divergence), (zones, heating - energy * divergence)):
            high, low = split_two(rate)
            rate_high_ref[rows, column : column + zones] = high
            rate_low_ref[rows, column : column + zones] = low
    nodal = 5 * ROWS
    main = mm(force_ref[...], high_ref[...])
    force = main[:nodal] + main[nodal:] + mm(force_ref[:nodal, :], low_ref[...])
    for comp in range(3):
        lanes = slice(zones * comp, zones * (comp + 1))
        for u in range(4):
            block = force[ROWS * u : ROWS * (u + 1), lanes]
            if u == 0:
                block = block + pltpu.roll(force[ROWS * 4 : ROWS * 5, lanes], 1, 1)
            lattice_ref[comp, :, zones * u : zones * (u + 1)] = block
    for comp in range(3):
        for s in range(5):
            face_up_ref[5 * comp + s, :] = lattice_ref[comp, 5 * s + 4, :]
            if face_down_ref is not None:
                face_down_ref[5 * comp + s, :] = lattice_ref[comp, 5 * s, :]
        edge_up_ref[5 * comp : 5 * comp + 5, :] = lattice_ref[comp, 20:25, :]
        if edge_down_ref is not None:
            edge_down_ref[5 * comp : 5 * comp + 5, :] = lattice_ref[comp, 0:5, :]
    main = mm(proj_ref[...], rate_high_ref[...])
    change = main[:MODES] + main[MODES:] + mm(proj_ref[:MODES, :], rate_low_ref[...])
    both = both + TIME_STEP * change
    modes_ref[:MODES, :] = both[:, :zones].astype(BF16)
    modes_ref[MODES:, :] = both[:, zones:].astype(BF16)


def zone_first_kernel(velocity_ref, mass_ref, halo_a_ref, halo_b_ref, halo_c_ref, fields_ref, grad_ref, force_ref,
                      inter_ref, proj_ref, state_ref, lattice_ref, up_ref, edge_up_ref, down_ref, edge_down_ref, modes_ref,
                      native_ref, *scratch):
    for comp in range(4):
        base = ROWS * comp
        native_ref[base + 24 : base + 32, :] = jnp.full((8, LINE), 1.0 if comp == 3 else 0.0, F32)
        for s in range(4):
            own = mass_ref[s] if comp == 3 else velocity_ref[comp, s]
            native_ref[base + 5 * s : base + 5 * s + 4, :] = own
            native_ref[base + 5 * s + 4, :] = halo_b_ref[comp, s, :]
        native_ref[base + 20 : base + 24, :] = halo_a_ref[comp]
        native_ref[base + 24, :] = halo_c_ref[comp, 0, :]
    selector = line_selector(True)
    count = 4 * ROWS
    for half in range(2):
        pieces = jnp.concatenate(split_three(native_ref[:, 512 * half : 512 * (half + 1)]), 0)
        moved = mm(pieces, selector)
        moved = moved[:count] + moved[count : 2 * count] + moved[2 * count :]
        for comp in range(4):
            for u in range(4):
                lanes = slice(256 * u + 128 * half, 256 * u + 128 * (half + 1))
                state_ref[comp, :, lanes] = moved[ROWS * comp : ROWS * (comp + 1), 128 * u : 128 * (u + 1)]
    modes = pick_modes(fields_ref[...])
    zone_math(lambda comp: state_ref[comp], modes, grad_ref, force_ref, inter_ref, proj_ref, *scratch,
              lattice_ref, up_ref, edge_up_ref, down_ref, edge_down_ref, modes_ref)


def add_faces(total_ref, low_ref, upper_ref):
    for comp in range(3):
        for s in range(5):
            at = 5 * comp + s
            total_ref[comp, 5 * s, :] = total_ref[comp, 5 * s, :] + low_ref[at, :]
            if upper_ref is not None:
                total_ref[comp, 5 * s + 4, :] = total_ref[comp, 5 * s + 4, :] + upper_ref[at, :]


def join_edge(block_ref):
    pair = block_ref[CAPACITY:FOLDED, :WIDTH].astype(F32)
    return pair[:, :LINE] + pair[:, LINE:]


def zone_second_kernel(state_ref, first_ref, low_ref, upper_ref, middle_ref, in_low_ref, in_upper_ref, grad_ref,
                       force_ref, inter_ref, proj_ref, fields_ref, total_ref, lattice_ref, up_ref, edge_up_ref,
                       modes_ref, edge_ref, *scratch):
    fields = sum_slots(middle_ref, in_low_ref, in_upper_ref)
    fields_ref[...] = fields
    total_ref[...] = first_ref[...]
    add_faces(total_ref, low_ref, upper_ref)
    for row, block_ref in ((0, in_low_ref), (20, in_upper_ref)):
        edge_ref[...] = join_edge(block_ref)
        for comp in range(3):
            at = slice(5 * comp, 5 * comp + 5)
            total_ref[comp, row : row + 5, :] = total_ref[comp, row : row + 5, :] + edge_ref[at, :]
    factor = TIME_STEP / state_ref[3]
    modes = pick_modes(fields)
    zone_math(lambda comp: state_ref[comp] - total_ref[comp] * factor, modes, grad_ref, force_ref, inter_ref,
              proj_ref, *scratch, lattice_ref, up_ref, edge_up_ref, None, None, modes_ref)


def sum_slots(*block_refs):
    incoming = jnp.concatenate([ref[:CAPACITY, :] for ref in block_refs], 0)
    codes = incoming[:, WIDTH:].astype(F32)
    label = iota((SLOTS, 128), 1).astype(F32)
    chosen = [jnp.where(codes == label + 128.0 * half, 1.0, 0.0).astype(BF16) for half in range(ZONE_COUNT // 128)]
    selector = jnp.concatenate(chosen, 1)
    return mm(selector, incoming[:, :WIDTH], ((0,), (0,))).astype(BF16)


def remap_kernel(step, fields_ref, modes_ref, matrix_ref, source_ref, target_ref, low_ref, middle_ref, upper_ref,
                 picked_ref, result_ref):
    zone = iota((ZONE_COUNT, SLOTS), 0)
    chosen = jnp.where(zone == source_ref[step : step + 1, :], 1.0, 0.0).astype(BF16)
    picked = mm(chosen, fields_ref[...], ((0,), (0,)))
    new = mm(chosen, modes_ref[...].T, ((0,), (0,))).astype(BF16)
    new = mm(new, mode_columns())
    lane = iota((SLOTS, 128), 1)
    group = lane // FIELDS
    renewed = lane % FIELDS < 2
    for g in range(WIDTH // 128):
        lanes = slice(128 * g, 128 * (g + 1))
        piece = jnp.where(renewed, new[:, lanes], picked[:, lanes])
        for r in range(4):
            picked_ref[pl.ds(4 * g + r, SLOTS, stride=MODES), :] = jnp.where(group == r, piece, 0.0)

    def multiply(trip, carry):
        for inner in range(8):
            slot = 8 * trip + inner
            at = pl.ds(pl.multiple_of(MODES * slot, MODES), MODES)
            result_ref[at, :] = mm(matrix_ref[0, slot], picked_ref[at, :].astype(BF16))
        return carry

    lax.fori_loop(0, SLOTS // 8, multiply, 0)
    outs = (low_ref, middle_ref, upper_ref)
    for g in range(WIDTH // 128):
        rows = [result_ref[pl.ds(4 * g + r, SLOTS, stride=MODES), :] for r in range(4)]
        total = None
        for shift in range(4):
            mixed = rows[3]
            for r in range(3):
                mixed = jnp.where(group == (r + shift) % 4, rows[r], mixed)
            if shift:
                mixed = pltpu.roll(mixed, 128 - FIELDS * shift, 1)
            total = mixed if total is None else total + mixed
        total = total.astype(BF16)
        for block in range(3):
            outs[block][:, 128 * g : 128 * (g + 1)] = total[CAPACITY * block : CAPACITY * (block + 1)]
    codes = jnp.broadcast_to(target_ref[step : step + 1, :].astype(F32), (8, SLOTS))
    codes = jnp.where(iota((8, SLOTS), 0) == 0, codes, 0.0).astype(BF16)
    codes = mm(codes, jnp.ones((8, 128), BF16), ((0,), (0,))).astype(BF16)
    for block in range(3):
        outs[block][:, WIDTH:] = codes[CAPACITY * block : CAPACITY * (block + 1)]


def fold_edge(edge_ref, source_row, low_ref, upper_ref, stage_ref, out_ref):
    stage_ref[15:16, :] = jnp.zeros((1, LINE), F32)
    stage_ref[0:15, :] = edge_ref[...]
    for comp in range(3):
        at = 5 * comp
        stage_ref[at, :] = stage_ref[at, :] + low_ref[at + source_row, :]
        if upper_ref is not None:
            stage_ref[at + 4, :] = stage_ref[at + 4, :] + upper_ref[at + source_row, :]
    high, low = split_two(stage_ref[...])
    out_ref[:, :LINE] = high
    out_ref[:, LINE:WIDTH] = low
    out_ref[:, WIDTH:] = jnp.zeros((16, 128), BF16)


def fold_first_kernel(up_any, down_any, edge_up_ref, edge_down_ref, low_ref, upper_ref, up_ref, down_ref, stage_ref):
    fold_edge(edge_up_ref, 4, low_ref, upper_ref, stage_ref, up_ref)
    fold_edge(edge_down_ref, 0, low_ref, upper_ref, stage_ref, down_ref)


def fold_second_kernel(up_any, edge_up_ref, low_ref, up_ref, stage_ref):
    fold_edge(edge_up_ref, 4, low_ref, None, stage_ref, up_ref)


def interleave(stage_ref, force_ref):
    count = stage_ref.shape[0]
    selector = line_selector(False)
    for half in range(2):
        grouped = jnp.concatenate(
            [stage_ref[:, 256 * u + 128 * half : 256 * u + 128 * (half + 1)] for u in range(4)], 1
        )
        moved = mm(jnp.concatenate(split_two(grouped), 0), selector)
        force_ref[:, 512 * half : 512 * (half + 1)] = moved[:count] + moved[count:]


def update_kernel(velocity_ref, displacement_ref, mass_ref, first_ref, second_ref, low_ref, velocity_out_ref,
                  displacement_out_ref, stage_ref, force_ref):
    for comp in range(3):
        for s in range(4):
            at = 16 * comp + 4 * s
            stage_ref[at : at + 4, :] = first_ref[comp, 5 * s : 5 * s + 4, :]
            stage_ref[48 + at : 48 + at + 4, :] = second_ref[comp, 5 * s : 5 * s + 4, :]
            stage_ref[48 + at, :] = stage_ref[48 + at, :] + low_ref[5 * comp + s, :]
    interleave(stage_ref, force_ref)
    for s in range(4):
        factor = TIME_STEP / mass_ref[s]
        for comp in range(3):
            at = 16 * comp + 4 * s
            middle = velocity_ref[comp, s] - force_ref[at : at + 4, :] * factor
            last = middle - force_ref[48 + at : 48 + at + 4, :] * factor
            velocity_out_ref[comp, s] = last
            displacement_out_ref[comp, s] = displacement_ref[comp, s] + TIME_STEP * middle + TIME_STEP * last


def finish_kernel(velocity_ref, displacement_ref, mass_ref, middle_ref, in_low_ref, in_upper_ref, fields_ref,
                  velocity_out_ref, displacement_out_ref, stage_ref, force_ref):
    fields_ref[...] = sum_slots(middle_ref, in_low_ref, in_upper_ref)
    stage_ref[...] = join_edge(in_low_ref)
    interleave(stage_ref, force_ref)
    factor = TIME_STEP / mass_ref[0]
    for comp in range(3):
        change = force_ref[5 * comp : 5 * comp + 4, :] * factor
        velocity_out_ref[comp, 0] = velocity_ref[comp, 0] - change
        displacement_out_ref[comp, 0] = displacement_ref[comp, 0] - TIME_STEP * change


def pack_kernel(velocity_ref, mass_ref, send_a_ref, send_b_ref, send_c_ref):
    for comp in range(4):
        for s in range(4):
            own = mass_ref[s] if comp == 3 else velocity_ref[comp, s]
            if s == 0:
                send_a_ref[comp] = own
                send_c_ref[comp] = own[:1]
            send_b_ref[comp, s : s + 1, :] = own[:1]


def shape(*dims, dtype=F32):
    return jax.ShapeDtypeStruct(dims, dtype)


LATTICE = (3, ROWS, LINE)
FACE = (15, LINE)


def zone_scratch():
    return [
        pltpu.VMEM((15 * ROWS, 3 * ZONE_COUNT), BF16),
        pltpu.VMEM((3 * POINTS, 3 * ZONE_COUNT), BF16),
        pltpu.VMEM((3 * POINTS, 3 * ZONE_COUNT), BF16),
        pltpu.VMEM((POINTS, 2 * ZONE_COUNT), BF16),
        pltpu.VMEM((POINTS, 2 * ZONE_COUNT), BF16),
    ]


def whole(*dims):
    return pl.BlockSpec(dims, lambda i: (0,) * len(dims))


def cost(microseconds):
    return pl.CostEstimate(flops=int(microseconds * 1e9), bytes_accessed=int(microseconds * 3e6), transcendentals=0)


ANYWHERE = pl.BlockSpec(memory_space=pl.ANY)
EDGE_BLOCK = pl.BlockSpec((16, SENT), lambda i: (CAPACITY // 16, 0))


def remap_call(step, fields, modes, matrix, source, target):
    return pl.pallas_call(
        lambda *refs: remap_kernel(step, *refs),
        grid=(1,),
        in_specs=[
            whole(ZONE_COUNT, WIDTH),
            whole(2 * MODES, ZONE_COUNT),
            whole(1, SLOTS, MODES, MODES),
            whole(STEPS, SLOTS),
            whole(STEPS, SLOTS),
        ],
        out_specs=[whole(CAPACITY, SENT)] * 3,
        out_shape=[shape(rows, SENT, dtype=BF16) for rows in (FOLDED if step == 0 else CAPACITY, CAPACITY, FOLDED)],
        scratch_shapes=[pltpu.VMEM((SLOTS * MODES, 128), F32)] * 2,
        cost_estimate=cost(9),
        name="remap_step",
    )(fields, modes, matrix[step : step + 1], source, target)


def body(fields, velocity, displacement, node_mass, remap_matrix, remap_source, remap_target):
    tables = basis_tables()
    lines = ("gx", "gy")
    send_a, send_b, send_c = pl.pallas_call(
        pack_kernel,
        out_shape=[shape(4, 4, LINE), shape(4, 4, LINE), shape(4, 1, LINE)],
        cost_estimate=cost(1),
        name="pack_halo",
    )(velocity, node_mass)
    size_a = lax.axis_size(lines)
    size_b = lax.axis_size("gz")
    corner = [
        (((i + 1) % size_a) * size_b + (j + 1) % size_b, i * size_b + j)
        for i in range(size_a)
        for j in range(size_b)
    ]
    halo_a = from_behind(send_a, lines, -1)
    halo_b = from_behind(send_b, "gz", -1)
    halo_c = lax.ppermute(send_c, ("gx", "gy", "gz"), corner)
    lattice = shape(*LATTICE)
    face = shape(*FACE)
    modes_shape = shape(2 * MODES, ZONE_COUNT, dtype=BF16)
    folded = shape(FOLDED, SENT, dtype=BF16)
    state, partial, up, edge_up, down, edge_down, modes = pl.pallas_call(
        zone_first_kernel,
        out_shape=[shape(4, ROWS, LINE), lattice, face, face, face, face, modes_shape],
        scratch_shapes=[pltpu.VMEM((4 * ROWS, LINE), F32)] + zone_scratch(),
        cost_estimate=cost(7),
        name="zone_first",
    )(velocity, node_mass, halo_a, halo_b, halo_c, fields, *tables)
    from_low = from_behind(up, "gz", 1)
    from_up = from_behind(down, "gz", -1)
    low, middle, upper = remap_call(0, fields, modes, remap_matrix, remap_source, remap_target)
    upper, low = pl.pallas_call(
        fold_first_kernel,
        grid=(1,),
        in_specs=[ANYWHERE, ANYWHERE] + [whole(*FACE)] * 4,
        out_specs=[EDGE_BLOCK, EDGE_BLOCK],
        out_shape=[folded, folded],
        input_output_aliases={0: 0, 1: 1},
        scratch_shapes=[pltpu.VMEM((16, LINE), F32)],
        cost_estimate=cost(1),
        name="fold_first",
    )(upper, low, edge_up, edge_down, from_low, from_up)
    in_low = from_behind(upper, lines, 1)
    in_upper = from_behind(low, lines, -1)
    fields, first, partial, up, edge_up, modes = pl.pallas_call(
        zone_second_kernel,
        out_shape=[shape(ZONE_COUNT, WIDTH, dtype=BF16), lattice, lattice, face, face, modes_shape],
        scratch_shapes=[pltpu.VMEM((16, LINE), F32)] + zone_scratch(),
        cost_estimate=cost(7),
        name="zone_second",
    )(state, partial, from_low, from_up, middle, in_low, in_upper, *tables)
    from_low = from_behind(up, "gz", 1)
    low, middle, upper = remap_call(1, fields, modes, remap_matrix, remap_source, remap_target)
    upper = pl.pallas_call(
        fold_second_kernel,
        grid=(1,),
        in_specs=[ANYWHERE] + [whole(*FACE)] * 2,
        out_specs=EDGE_BLOCK,
        out_shape=folded,
        input_output_aliases={0: 0},
        scratch_shapes=[pltpu.VMEM((16, LINE), F32)],
        cost_estimate=cost(1),
        name="fold_second",
    )(upper, edge_up, from_low)
    in_upper = from_behind(low, lines, -1)
    in_low = from_behind(upper, lines, 1)
    nodal = shape(*velocity.shape)
    velocity_part, displacement_part = pl.pallas_call(
        update_kernel,
        out_shape=[nodal, nodal],
        scratch_shapes=[pltpu.VMEM((96, LINE), F32)] * 2,
        cost_estimate=cost(2.5),
        name="update_nodes",
    )(velocity, displacement, node_mass, first, partial, from_low)
    bottom = whole(3, 1, 4, LINE)
    fields_out, velocity_out, displacement_out = pl.pallas_call(
        finish_kernel,
        grid=(1,),
        in_specs=[
            bottom,
            bottom,
            whole(1, 4, LINE),
            whole(CAPACITY, SENT),
            whole(FOLDED, SENT),
            whole(CAPACITY, SENT),
        ],
        out_specs=[whole(ZONE_COUNT, WIDTH), bottom, bottom],
        out_shape=[shape(ZONE_COUNT, WIDTH, dtype=BF16), nodal, nodal],
        input_output_aliases={0: 1, 1: 2},
        scratch_shapes=[pltpu.VMEM((16, LINE), F32)] * 2,
        cost_estimate=cost(3),
        name="finish_step",
    )(velocity_part, displacement_part, node_mass, middle, in_low, in_upper)
    return (fields_out, velocity_out, displacement_out)


def solution(mesh):
    in_specs = (
        P(("gx", "gy", "gz"), None),
        P(None, ("gx", "gy"), "gz", None),
        P(None, ("gx", "gy"), "gz", None),
        P(("gx", "gy"), "gz", None),
        P(None, ("gx", "gy", "gz"), None, None),
        P(None, ("gx", "gy", "gz")),
        P(None, ("gx", "gy", "gz")),
    )
    out_specs = (
        P(("gx", "gy", "gz"), None),
        P(None, ("gx", "gy"), "gz", None),
        P(None, ("gx", "gy"), "gz", None),
    )
    return jax.shard_map(body, mesh=mesh, in_specs=in_specs, out_specs=out_specs, check_vma=False)
```

```python
import math

import jax
import jax.numpy as jnp
import numpy as np
from jax import lax
from jax.experimental import pallas as pl
from jax.experimental.pallas import tpu as pltpu
from jax.sharding import PartitionSpec as P

NODES = 125
POINTS = 512
MODES = 64
FIELDS = 32
STEPS = 2


TIME_STEP = 0.3
GAMMA_LESS = 0.4
VISCOSITY = 0.3
F32 = jnp.float32
BF16 = jnp.bfloat16
ZONE_COUNT = 256
ROWS = 32
LINE = 1024
CAPACITY = 32
SLOTS = 96
WIDTH = MODES * FIELDS
SENT = WIDTH + 128
FOLDED = CAPACITY + 16


def from_behind(shard, axis, by):
    size = lax.axis_size(axis)
    return lax.ppermute(shard, axis, [(i, (i + by) % size) for i in range(size)])


def gauss_rule(order):
    if order == 8:
        half_points = [
            0.1834346424956498,
            0.525532409916329,
            0.7966664774136267,
            0.9602898564975363,
        ]
        half_weights = [
            0.362683783378362,
            0.3137066458778873,
            0.2223810344533745,
            0.1012285362903763,
        ]
    else:
        half_points = [0.3399810435848563, 0.8611363115940526]
        half_weights = [0.6521451548625461, 0.3478548451374538]
    points = np.array([-value for value in half_points[::-1]] + half_points)
    weights = np.array(half_weights[::-1] + half_weights)
    return (points, weights)


def lagrange_tables(nodes, points):
    values = np.ones((points.shape[0], nodes.shape[0]))
    slopes = np.zeros((points.shape[0], nodes.shape[0]))
    for column in range(nodes.shape[0]):
        for other in range(nodes.shape[0]):
            if other != column:
                values[:, column] *= (points - nodes[other]) / (nodes[column] - nodes[other])
        for other in range(nodes.shape[0]):
            if other != column:
                product = np.ones(points.shape) / (nodes[column] - nodes[other])
                for third in range(nodes.shape[0]):
                    if third != column and third != other:
                        product = product * (points - nodes[third]) / (nodes[column] - nodes[third])
                slopes[:, column] += product
    return (values, slopes)


def kron_three(first, second, third):
    return np.kron(np.kron(first, second), third)


def split_table(table):
    high = table.astype(jnp.bfloat16)
    low = (table - high.astype(np.float32)).astype(jnp.bfloat16)
    return (high, low)


def node_columns(table):
    grid = table.reshape(-1, 5, 25 // 5, 5).transpose(0, 3, 1, 2).reshape(-1, 5, 25)
    return np.pad(grid, ((0, 0), (0, 0), (0, ROWS - 25))).reshape(-1, 5 * ROWS)


def basis_tables():
    gauss_points, gauss_weights = gauss_rule(8)
    points = (gauss_points + 1.0) / 2.0
    weights = gauss_weights / 2.0
    root = math.sqrt(3.0 / 7.0)
    lobatto = (np.array([-1.0, -root, 0.0, root, 1.0]) + 1.0) / 2.0
    four_points, four_weights = gauss_rule(4)
    legendre_nodes = (four_points + 1.0) / 2.0
    node_values, node_slopes = lagrange_tables(lobatto, points)
    mode_values, unused_slopes = lagrange_tables(legendre_nodes, points)
    gradient_table = np.concatenate(
        [
            kron_three(node_slopes, node_values, node_values),
            kron_three(node_values, node_slopes, node_values),
            kron_three(node_values, node_values, node_slopes),
        ],
        0,
    )
    interpolate = kron_three(mode_values, mode_values, mode_values)
    weight_table = kron_three(weights, weights, weights)
    mass_diagonal = four_weights / 2.0
    project_line = mode_values.T * weights[None, :] / mass_diagonal[:, None]
    projection = kron_three(project_line, project_line, project_line)
    gradient_table = gradient_table.astype(np.float32)
    weighted_table = gradient_table * np.tile(weight_table.astype(np.float32), 3)[:, None]
    grad_hi, grad_lo = split_table(node_columns(gradient_table))
    force_hi, force_lo = split_table(node_columns(weighted_table).T)
    inter_hi, inter_lo = split_table(interpolate.astype(np.float32))
    proj_hi, proj_lo = split_table(projection.astype(np.float32))
    return (
        jnp.asarray(np.concatenate([grad_hi, grad_hi, grad_lo], 1)),
        jnp.asarray(np.concatenate([force_hi, force_lo], 0)),
        jnp.asarray(np.concatenate([inter_hi, inter_lo], 1)),
        jnp.asarray(np.concatenate([proj_hi, proj_lo], 0)),
    )


def split_two(values):
    high = values.astype(BF16)
    return (high, (values - high.astype(F32)).astype(BF16))


def split_three(values):
    high = values.astype(BF16)
    rest = values - high.astype(F32)
    middle = rest.astype(BF16)
    return (high, middle, (rest - middle.astype(F32)).astype(BF16))


def mm(left, right, dims=((1,), (0,))):
    return lax.dot_general(left, right, (dims, ((), ())), preferred_element_type=F32)


def iota(shape, axis):
    return lax.broadcasted_iota(jnp.int32, shape, axis)


def line_selector(to_zones):
    lattice = iota((512, 512), 0 if to_zones else 1)
    grouped = iota((512, 512), 1 if to_zones else 0)
    return jnp.where(4 * (grouped % 128) + grouped // 128 == lattice, 1.0, 0.0).astype(BF16)


def mode_columns():
    row = iota((2 * MODES, WIDTH), 0)
    column = iota((2 * MODES, WIDTH), 1)
    return jnp.where(FIELDS * (row % MODES) + row // MODES == column, 1.0, 0.0).astype(BF16)


def pick_modes(fields):
    return mm(mode_columns(), fields, ((1,), (1,)))


def zone_math(velocity_of, modes, grad_ref, force_ref, inter_ref, proj_ref, nodes_ref, high_ref, low_ref,
              rate_high_ref, rate_low_ref, lattice_ref, face_up_ref, edge_up_ref, face_down_ref, edge_down_ref, modes_ref):
    zones = ZONE_COUNT
    for comp in range(3):
        line = velocity_of(comp)
        lanes = slice(zones * comp, zones * (comp + 1))
        groups = [line[:, zones * u : zones * (u + 1)] for u in range(4)]
        groups.append(pltpu.roll(groups[0], zones - 1, 1))
        for u in range(5):
            high, low = split_two(groups[u])
            nodes_ref[ROWS * u : ROWS * (u + 1), lanes] = high
            nodes_ref[ROWS * (5 + u) : ROWS * (6 + u), lanes] = low
            nodes_ref[ROWS * (10 + u) : ROWS * (11 + u), lanes] = high
    both = jnp.concatenate([modes[:MODES], modes[MODES:]], 1)
    twice = jnp.concatenate([both, both], 0).astype(BF16)
    chunk = 128
    for part in range(POINTS // chunk):
        rows = slice(chunk * part, chunk * (part + 1))
        nodes = nodes_ref[...]
        grads = []
        for first in range(3):
            start = POINTS * first + chunk * part
            flat = mm(grad_ref[start : start + chunk, :], nodes)
            grads.append([flat[:, zones * c : zones * (c + 1)] for c in range(3)])
        points = mm(inter_ref[rows, :], twice)
        rho = points[:, :zones]
        energy = points[:, zones:]
        divergence = grads[0][0] + grads[1][1] + grads[2][2]
        pressure = GAMMA_LESS * energy
        viscous = 0.5 * VISCOSITY * rho
        heating = None
        for first in range(3):
            for second in range(first, 3):
                total = grads[first][second] + grads[second][first]
                entry = viscous * total
                if first == second:
                    entry = entry - pressure
                    work = entry * grads[first][first]
                else:
                    work = entry * total
                heating = work if heating is None else heating + work
                high, low = split_two(entry)
                for d, c in ((first, second), (second, first))[: 1 if first == second else 2]:
                    at = slice(POINTS * d + chunk * part, POINTS * d + chunk * (part + 1))
                    lanes = slice(zones * c, zones * (c + 1))
                    high_ref[at, lanes] = high
                    low_ref[at, lanes] = low
        for column, rate in ((0, -rho * divergence), (zones, heating - energy * divergence)):
            high, low = split_two(rate)
            rate_high_ref[rows, column : column + zones] = high
            rate_low_ref[rows, column : column + zones] = low
    nodal = 5 * ROWS
    main = mm(force_ref[...], high_ref[...])
    force = main[:nodal] + main[nodal:] + mm(force_ref[:nodal, :], low_ref[...])
    for comp in range(3):
        lanes = slice(zones * comp, zones * (comp + 1))
        for u in range(4):
            block = force[ROWS * u : ROWS * (u + 1), lanes]
            if u == 0:
                block = block + pltpu.roll(force[ROWS * 4 : ROWS * 5, lanes], 1, 1)
            lattice_ref[comp, :, zones * u : zones * (u + 1)] = block
    for comp in range(3):
        for s in range(5):
            face_up_ref[5 * comp + s, :] = lattice_ref[comp, 5 * s + 4, :]
            if face_down_ref is not None:
                face_down_ref[5 * comp + s, :] = lattice_ref[comp, 5 * s, :]
        edge_up_ref[5 * comp : 5 * comp + 5, :] = lattice_ref[comp, 20:25, :]
        if edge_down_ref is not None:
            edge_down_ref[5 * comp : 5 * comp + 5, :] = lattice_ref[comp, 0:5, :]
    main = mm(proj_ref[...], rate_high_ref[...])
    change = main[:MODES] + main[MODES:] + mm(proj_ref[:MODES, :], rate_low_ref[...])
    both = both + TIME_STEP * change
    modes_ref[:MODES, :] = both[:, :zones].astype(BF16)
    modes_ref[MODES:, :] = both[:, zones:].astype(BF16)


def zone_first_kernel(velocity_ref, mass_ref, halo_a_ref, halo_b_ref, halo_c_ref, fields_ref, grad_ref, force_ref,
                      inter_ref, proj_ref, state_ref, lattice_ref, up_ref, edge_up_ref, down_ref, edge_down_ref, modes_ref,
                      native_ref, *scratch):
    for comp in range(4):
        base = ROWS * comp
        native_ref[base + 24 : base + 32, :] = jnp.full((8, LINE), 1.0 if comp == 3 else 0.0, F32)
        for s in range(4):
            own = mass_ref[s] if comp == 3 else velocity_ref[comp, s]
            native_ref[base + 5 * s : base + 5 * s + 4, :] = own
            native_ref[base + 5 * s + 4, :] = halo_b_ref[comp, s, :]
        native_ref[base + 20 : base + 24, :] = halo_a_ref[comp]
        native_ref[base + 24, :] = halo_c_ref[comp, 0, :]
    selector = line_selector(True)
    count = 4 * ROWS
    for half in range(2):
        pieces = jnp.concatenate(split_three(native_ref[:, 512 * half : 512 * (half + 1)]), 0)
        moved = mm(pieces, selector)
        moved = moved[:count] + moved[count : 2 * count] + moved[2 * count :]
        for comp in range(4):
            for u in range(4):
                lanes = slice(256 * u + 128 * half, 256 * u + 128 * (half + 1))
                state_ref[comp, :, lanes] = moved[ROWS * comp : ROWS * (comp + 1), 128 * u : 128 * (u + 1)]
    modes = pick_modes(fields_ref[...])
    zone_math(lambda comp: state_ref[comp], modes, grad_ref, force_ref, inter_ref, proj_ref, *scratch,
              lattice_ref, up_ref, edge_up_ref, down_ref, edge_down_ref, modes_ref)


def add_faces(total_ref, low_ref, upper_ref):
    for comp in range(3):
        for s in range(5):
            at = 5 * comp + s
            total_ref[comp, 5 * s, :] = total_ref[comp, 5 * s, :] + low_ref[at, :]
            if upper_ref is not None:
                total_ref[comp, 5 * s + 4, :] = total_ref[comp, 5 * s + 4, :] + upper_ref[at, :]


def join_edge(block_ref):
    pair = block_ref[CAPACITY:FOLDED, :WIDTH].astype(F32)
    return pair[:, :LINE] + pair[:, LINE:]


def zone_second_kernel(state_ref, first_ref, low_ref, upper_ref, middle_ref, in_low_ref, in_upper_ref, grad_ref,
                       force_ref, inter_ref, proj_ref, fields_ref, total_ref, lattice_ref, up_ref, edge_up_ref,
                       modes_ref, edge_ref, *scratch):
    fields = sum_slots(middle_ref, in_low_ref, in_upper_ref)
    fields_ref[...] = fields
    total_ref[...] = first_ref[...]
    add_faces(total_ref, low_ref, upper_ref)
    for row, block_ref in ((0, in_low_ref), (20, in_upper_ref)):
        edge_ref[...] = join_edge(block_ref)
        for comp in range(3):
            at = slice(5 * comp, 5 * comp + 5)
            total_ref[comp, row : row + 5, :] = total_ref[comp, row : row + 5, :] + edge_ref[at, :]
    factor = TIME_STEP / state_ref[3]
    modes = pick_modes(fields)
    zone_math(lambda comp: state_ref[comp] - total_ref[comp] * factor, modes, grad_ref, force_ref, inter_ref,
              proj_ref, *scratch, lattice_ref, up_ref, edge_up_ref, None, None, modes_ref)


def sum_slots(*block_refs):
    incoming = jnp.concatenate([ref[:CAPACITY, :] for ref in block_refs], 0)
    codes = incoming[:, WIDTH:].astype(F32)
    label = iota((SLOTS, 128), 1).astype(F32)
    chosen = [jnp.where(codes == label + 128.0 * half, 1.0, 0.0).astype(BF16) for half in range(ZONE_COUNT // 128)]
    selector = jnp.concatenate(chosen, 1)
    return mm(selector, incoming[:, :WIDTH], ((0,), (0,))).astype(BF16)


def remap_kernel(step, blocks, fields_ref, modes_ref, source_ref, target_ref, *refs):
    number = len(blocks)
    matrix_refs, outs = refs[:number], refs[number : 2 * number]
    picked_ref, result_ref = refs[2 * number :]
    slots = CAPACITY * number

    def slots_of(ref):
        pieces = [ref[step : step + 1, CAPACITY * block : CAPACITY * (block + 1)] for block in blocks]
        return pieces[0] if number == 1 else jnp.concatenate(pieces, 1)

    zone = iota((ZONE_COUNT, slots), 0)
    chosen = jnp.where(zone == slots_of(source_ref), 1.0, 0.0).astype(BF16)
    picked = mm(chosen, fields_ref[...], ((0,), (0,)))
    new = mm(chosen, modes_ref[...].T, ((0,), (0,))).astype(BF16)
    new = mm(new, mode_columns())
    lane = iota((slots, 128), 1)
    group = lane // FIELDS
    renewed = lane % FIELDS < 2
    for g in range(WIDTH // 128):
        lanes = slice(128 * g, 128 * (g + 1))
        piece = jnp.where(renewed, new[:, lanes], picked[:, lanes])
        for r in range(4):
            picked_ref[pl.ds(4 * g + r, slots, stride=MODES), :] = jnp.where(group == r, piece, 0.0)
    for place, matrix_ref in enumerate(matrix_refs):

        def multiply(trip, carry):
            for inner in range(16):
                slot = 16 * trip + inner
                at = pl.ds(pl.multiple_of(MODES * (CAPACITY * place + slot), MODES), MODES)
                result_ref[at, :] = mm(matrix_ref[0, slot], picked_ref[at, :].astype(BF16))
            return carry

        lax.fori_loop(0, CAPACITY // 16, multiply, 0)
    for g in range(WIDTH // 128):
        rows = [result_ref[pl.ds(4 * g + r, slots, stride=MODES), :] for r in range(4)]
        total = None
        for shift in range(4):
            mixed = rows[3]
            for r in range(3):
                mixed = jnp.where(group == (r + shift) % 4, rows[r], mixed)
            if shift:
                mixed = pltpu.roll(mixed, 128 - FIELDS * shift, 1)
            total = mixed if total is None else total + mixed
        total = total.astype(BF16)
        for place in range(number):
            outs[place][:, 128 * g : 128 * (g + 1)] = total[CAPACITY * place : CAPACITY * (place + 1)]
    codes = jnp.broadcast_to(slots_of(target_ref).astype(F32), (8, slots))
    codes = jnp.where(iota((8, slots), 0) == 0, codes, 0.0).astype(BF16)
    codes = mm(codes, jnp.ones((8, 128), BF16), ((0,), (0,))).astype(BF16)
    for place in range(number):
        outs[place][:, WIDTH:] = codes[CAPACITY * place : CAPACITY * (place + 1)]


def fold_edge(edge_ref, source_row, low_ref, upper_ref, stage_ref, out_ref):
    stage_ref[15:16, :] = jnp.zeros((1, LINE), F32)
    stage_ref[0:15, :] = edge_ref[...]
    for comp in range(3):
        at = 5 * comp
        stage_ref[at, :] = stage_ref[at, :] + low_ref[at + source_row, :]
        if upper_ref is not None:
            stage_ref[at + 4, :] = stage_ref[at + 4, :] + upper_ref[at + source_row, :]
    high, low = split_two(stage_ref[...])
    out_ref[:, :LINE] = high
    out_ref[:, LINE:WIDTH] = low
    out_ref[:, WIDTH:] = jnp.zeros((16, 128), BF16)


def fold_first_kernel(up_any, down_any, edge_up_ref, edge_down_ref, low_ref, upper_ref, up_ref, down_ref, stage_ref):
    fold_edge(edge_up_ref, 4, low_ref, upper_ref, stage_ref, up_ref)
    fold_edge(edge_down_ref, 0, low_ref, upper_ref, stage_ref, down_ref)


def fold_second_kernel(up_any, down_any, edge_up_ref, low_ref, up_ref, down_ref, stage_ref):
    fold_edge(edge_up_ref, 4, low_ref, None, stage_ref, up_ref)


def interleave(stage_ref, force_ref):
    count = stage_ref.shape[0]
    selector = line_selector(False)
    for half in range(2):
        grouped = jnp.concatenate(
            [stage_ref[:, 256 * u + 128 * half : 256 * u + 128 * (half + 1)] for u in range(4)], 1
        )
        moved = mm(jnp.concatenate(split_two(grouped), 0), selector)
        force_ref[:, 512 * half : 512 * (half + 1)] = moved[:count] + moved[count:]


def update_kernel(velocity_ref, displacement_ref, mass_ref, first_ref, second_ref, low_ref, velocity_out_ref,
                  displacement_out_ref, stage_ref, force_ref):
    for comp in range(3):
        for s in range(4):
            at = 16 * comp + 4 * s
            stage_ref[at : at + 4, :] = first_ref[comp, 5 * s : 5 * s + 4, :]
            stage_ref[48 + at : 48 + at + 4, :] = second_ref[comp, 5 * s : 5 * s + 4, :]
            stage_ref[48 + at, :] = stage_ref[48 + at, :] + low_ref[5 * comp + s, :]
    interleave(stage_ref, force_ref)
    for s in range(4):
        factor = TIME_STEP / mass_ref[s]
        for comp in range(3):
            at = 16 * comp + 4 * s
            middle = velocity_ref[comp, s] - force_ref[at : at + 4, :] * factor
            last = middle - force_ref[48 + at : 48 + at + 4, :] * factor
            velocity_out_ref[comp, s] = last
            displacement_out_ref[comp, s] = displacement_ref[comp, s] + TIME_STEP * middle + TIME_STEP * last


def finish_kernel(velocity_ref, displacement_ref, mass_ref, middle_ref, in_low_ref, in_upper_ref, fields_ref,
                  velocity_out_ref, displacement_out_ref, stage_ref, force_ref):
    fields_ref[...] = sum_slots(middle_ref, in_low_ref, in_upper_ref)
    stage_ref[...] = join_edge(in_low_ref)
    interleave(stage_ref, force_ref)
    factor = TIME_STEP / mass_ref[0]
    for comp in range(3):
        change = force_ref[5 * comp : 5 * comp + 4, :] * factor
        velocity_out_ref[comp, 0] = velocity_ref[comp, 0] - change
        displacement_out_ref[comp, 0] = displacement_ref[comp, 0] - TIME_STEP * change


def pack_kernel(velocity_ref, mass_ref, send_a_ref, send_b_ref, send_c_ref):
    for comp in range(4):
        for s in range(4):
            own = mass_ref[s] if comp == 3 else velocity_ref[comp, s]
            if s == 0:
                send_a_ref[comp] = own
                send_c_ref[comp] = own[:1]
            send_b_ref[comp, s : s + 1, :] = own[:1]


def shape(*dims, dtype=F32):
    return jax.ShapeDtypeStruct(dims, dtype)


LATTICE = (3, ROWS, LINE)
FACE = (15, LINE)


def zone_scratch():
    return [
        pltpu.VMEM((15 * ROWS, 3 * ZONE_COUNT), BF16),
        pltpu.VMEM((3 * POINTS, 3 * ZONE_COUNT), BF16),
        pltpu.VMEM((3 * POINTS, 3 * ZONE_COUNT), BF16),
        pltpu.VMEM((POINTS, 2 * ZONE_COUNT), BF16),
        pltpu.VMEM((POINTS, 2 * ZONE_COUNT), BF16),
    ]


def whole(*dims):
    return pl.BlockSpec(dims, lambda i: (0,) * len(dims))


def cost(microseconds):
    return pl.CostEstimate(flops=int(microseconds * 1e9), bytes_accessed=int(microseconds * 3e6), transcendentals=0)


LIMIT = pltpu.CompilerParams(vmem_limit_bytes=40 * 1024 * 1024)
ANYWHERE = pl.BlockSpec(memory_space=pl.ANY)
EDGE_BLOCK = pl.BlockSpec((16, SENT), lambda i: (CAPACITY // 16, 0))


def remap_call(step, blocks, rows, fields, modes, matrix, source, target):
    return pl.pallas_call(
        lambda *refs: remap_kernel(step, blocks, *refs),
        grid=(1,),
        in_specs=[whole(ZONE_COUNT, WIDTH), whole(2 * MODES, ZONE_COUNT), whole(STEPS, SLOTS), whole(STEPS, SLOTS)]
        + [pl.BlockSpec((1, CAPACITY, MODES, MODES), lambda i, block=block: (0, block, 0, 0)) for block in blocks],
        out_specs=[whole(CAPACITY, SENT)] * len(blocks),
        out_shape=[shape(count, SENT, dtype=BF16) for count in rows],
        scratch_shapes=[pltpu.VMEM((CAPACITY * len(blocks) * MODES, 128), F32)] * 2,
        compiler_params=LIMIT,
        cost_estimate=cost(3 * len(blocks)),
        name="remap_step",
    )(fields, modes, source, target, *[matrix] * len(blocks))


def near(*arrays):
    return [pltpu.with_memory_space_constraint(array, pltpu.VMEM) for array in arrays]


def body(fields, velocity, displacement, node_mass, remap_matrix, remap_source, remap_target):
    tables = basis_tables()
    lines = ("gx", "gy")
    send_a, send_b, send_c = pl.pallas_call(
        pack_kernel,
        out_shape=[shape(4, 4, LINE), shape(4, 4, LINE), shape(4, 1, LINE)],
        compiler_params=LIMIT,
        cost_estimate=cost(1),
        name="pack_halo",
    )(velocity, node_mass)
    size_a = lax.axis_size(lines)
    size_b = lax.axis_size("gz")
    corner = [
        (((i + 1) % size_a) * size_b + (j + 1) % size_b, i * size_b + j)
        for i in range(size_a)
        for j in range(size_b)
    ]
    halo_a = from_behind(send_a, lines, -1)
    halo_b = from_behind(send_b, "gz", -1)
    halo_c = lax.ppermute(send_c, ("gx", "gy", "gz"), corner)
    lattice = shape(*LATTICE)
    face = shape(*FACE)
    modes_shape = shape(2 * MODES, ZONE_COUNT, dtype=BF16)
    folded = shape(FOLDED, SENT, dtype=BF16)
    state, partial, up, edge_up, down, edge_down, modes = pl.pallas_call(
        zone_first_kernel,
        out_shape=[shape(4, ROWS, LINE), lattice, face, face, face, face, modes_shape],
        scratch_shapes=[pltpu.VMEM((4 * ROWS, LINE), F32)] + zone_scratch(),
        compiler_params=LIMIT,
        cost_estimate=cost(7),
        name="zone_first",
    )(velocity, node_mass, *near(halo_a, halo_b, halo_c), fields, *near(*tables))
    from_low = from_behind(up, "gz", 1)
    from_up = from_behind(down, "gz", -1)
    index = (remap_source, remap_target)
    matrix = remap_matrix[0:1]
    low, upper = remap_call(0, (0, 2), (FOLDED, FOLDED), fields, modes, matrix, *index)
    upper, low = pl.pallas_call(
        fold_first_kernel,
        grid=(1,),
        in_specs=[ANYWHERE, ANYWHERE] + [whole(*FACE)] * 4,
        out_specs=[EDGE_BLOCK, EDGE_BLOCK],
        out_shape=[folded, folded],
        input_output_aliases={0: 0, 1: 1},
        scratch_shapes=[pltpu.VMEM((16, LINE), F32)],
        compiler_params=LIMIT,
        cost_estimate=cost(1),
        name="fold_first",
    )(upper, low, edge_up, edge_down, *near(from_low, from_up))
    near_fields, modes, upper, low = lax.optimization_barrier((fields, modes, upper, low))
    in_low = from_behind(upper, lines, 1)
    in_upper = from_behind(low, lines, -1)
    (middle,) = remap_call(0, (1,), (CAPACITY,), near_fields, modes, matrix, *index)
    fields, first, partial, up, edge_up, modes = pl.pallas_call(
        zone_second_kernel,
        out_shape=[shape(ZONE_COUNT, WIDTH, dtype=BF16), lattice, lattice, face, face, modes_shape],
        scratch_shapes=[pltpu.VMEM((16, LINE), F32)] + zone_scratch(),
        compiler_params=LIMIT,
        cost_estimate=cost(7),
        name="zone_second",
    )(state, partial, *near(from_low, from_up), middle, *near(in_low, in_upper, *tables))
    from_low = from_behind(up, "gz", 1)
    matrix = remap_matrix[1:2]
    low, upper = remap_call(1, (0, 2), (CAPACITY, FOLDED), fields, modes, matrix, *index)
    upper, low = pl.pallas_call(
        fold_second_kernel,
        grid=(1,),
        in_specs=[ANYWHERE, ANYWHERE] + [whole(*FACE)] * 2,
        out_specs=[EDGE_BLOCK, ANYWHERE],
        out_shape=[folded, shape(CAPACITY, SENT, dtype=BF16)],
        input_output_aliases={0: 0, 1: 1},
        scratch_shapes=[pltpu.VMEM((16, LINE), F32)],
        compiler_params=LIMIT,
        cost_estimate=cost(1),
        name="fold_second",
    )(upper, low, edge_up, *near(from_low))
    fields, modes, upper, low = lax.optimization_barrier((fields, modes, upper, low))
    in_upper = from_behind(low, lines, -1)
    in_low = from_behind(upper, lines, 1)
    (middle,) = remap_call(1, (1,), (CAPACITY,), fields, modes, matrix, *index)
    nodal = shape(*velocity.shape)
    velocity_part, displacement_part = pl.pallas_call(
        update_kernel,
        out_shape=[nodal, nodal],
        scratch_shapes=[pltpu.VMEM((96, LINE), F32)] * 2,
        compiler_params=LIMIT,
        cost_estimate=cost(2.5),
        name="update_nodes",
    )(velocity, displacement, node_mass, first, partial, *near(from_low))
    bottom = whole(3, 1, 4, LINE)
    fields_out, velocity_out, displacement_out = pl.pallas_call(
        finish_kernel,
        grid=(1,),
        in_specs=[
            bottom,
            bottom,
            whole(1, 4, LINE),
            whole(CAPACITY, SENT),
            whole(FOLDED, SENT),
            whole(CAPACITY, SENT),
        ],
        out_specs=[whole(ZONE_COUNT, WIDTH), bottom, bottom],
        out_shape=[shape(ZONE_COUNT, WIDTH, dtype=BF16), nodal, nodal],
        input_output_aliases={0: 1, 1: 2},
        scratch_shapes=[pltpu.VMEM((16, LINE), F32)] * 2,
        compiler_params=LIMIT,
        cost_estimate=cost(3),
        name="finish_step",
    )(velocity_part, displacement_part, node_mass, middle, *near(in_low, in_upper))
    return (fields_out, velocity_out, displacement_out)


def solution(mesh):
    in_specs = (
        P(("gx", "gy", "gz"), None),
        P(None, ("gx", "gy"), "gz", None),
        P(None, ("gx", "gy"), "gz", None),
        P(("gx", "gy"), "gz", None),
        P(None, ("gx", "gy", "gz"), None, None),
        P(None, ("gx", "gy", "gz")),
        P(None, ("gx", "gy", "gz")),
    )
    out_specs = (
        P(("gx", "gy", "gz"), None),
        P(None, ("gx", "gy"), "gz", None),
        P(None, ("gx", "gy"), "gz", None),
    )
    return jax.shard_map(body, mesh=mesh, in_specs=in_specs, out_specs=out_specs, check_vma=False)
```

```python
import math

import jax
import jax.numpy as jnp
import numpy as np
from jax import lax
from jax.experimental import pallas as pl
from jax.experimental.pallas import tpu as pltpu
from jax.sharding import PartitionSpec as P

NODES = 125
POINTS = 512
MODES = 64
FIELDS = 32
STEPS = 2


TIME_STEP = 0.3
GAMMA_LESS = 0.4
VISCOSITY = 0.3
F32 = jnp.float32
BF16 = jnp.bfloat16
ZONE_COUNT = 256
ROWS = 32
LINE = 1024
CAPACITY = 32
SLOTS = 96
WIDTH = MODES * FIELDS
SENT = WIDTH + 128
FOLDED = CAPACITY + 16


def from_behind(shard, axis, by):
    size = lax.axis_size(axis)
    return lax.ppermute(shard, axis, [(i, (i + by) % size) for i in range(size)])


def gauss_rule(order):
    if order == 8:
        half_points = [
            0.1834346424956498,
            0.525532409916329,
            0.7966664774136267,
            0.9602898564975363,
        ]
        half_weights = [
            0.362683783378362,
            0.3137066458778873,
            0.2223810344533745,
            0.1012285362903763,
        ]
    else:
        half_points = [0.3399810435848563, 0.8611363115940526]
        half_weights = [0.6521451548625461, 0.3478548451374538]
    points = np.array([-value for value in half_points[::-1]] + half_points)
    weights = np.array(half_weights[::-1] + half_weights)
    return (points, weights)


def lagrange_tables(nodes, points):
    values = np.ones((points.shape[0], nodes.shape[0]))
    slopes = np.zeros((points.shape[0], nodes.shape[0]))
    for column in range(nodes.shape[0]):
        for other in range(nodes.shape[0]):
            if other != column:
                values[:, column] *= (points - nodes[other]) / (nodes[column] - nodes[other])
        for other in range(nodes.shape[0]):
            if other != column:
                product = np.ones(points.shape) / (nodes[column] - nodes[other])
                for third in range(nodes.shape[0]):
                    if third != column and third != other:
                        product = product * (points - nodes[third]) / (nodes[column] - nodes[third])
                slopes[:, column] += product
    return (values, slopes)


def kron_three(first, second, third):
    return np.kron(np.kron(first, second), third)


def split_table(table):
    high = table.astype(jnp.bfloat16)
    low = (table - high.astype(np.float32)).astype(jnp.bfloat16)
    return (high, low)


def node_columns(table):
    grid = table.reshape(-1, 5, 25 // 5, 5).transpose(0, 3, 1, 2).reshape(-1, 5, 25)
    return np.pad(grid, ((0, 0), (0, 0), (0, ROWS - 25))).reshape(-1, 5 * ROWS)


def basis_tables():
    gauss_points, gauss_weights = gauss_rule(8)
    points = (gauss_points + 1.0) / 2.0
    weights = gauss_weights / 2.0
    root = math.sqrt(3.0 / 7.0)
    lobatto = (np.array([-1.0, -root, 0.0, root, 1.0]) + 1.0) / 2.0
    four_points, four_weights = gauss_rule(4)
    legendre_nodes = (four_points + 1.0) / 2.0
    node_values, node_slopes = lagrange_tables(lobatto, points)
    mode_values, unused_slopes = lagrange_tables(legendre_nodes, points)
    gradient_table = np.concatenate(
        [
            kron_three(node_slopes, node_values, node_values),
            kron_three(node_values, node_slopes, node_values),
            kron_three(node_values, node_values, node_slopes),
        ],
        0,
    )
    interpolate = kron_three(mode_values, mode_values, mode_values)
    weight_table = kron_three(weights, weights, weights)
    mass_diagonal = four_weights / 2.0
    project_line = mode_values.T * weights[None, :] / mass_diagonal[:, None]
    projection = kron_three(project_line, project_line, project_line)
    gradient_table = gradient_table.astype(np.float32)
    weighted_table = gradient_table * np.tile(weight_table.astype(np.float32), 3)[:, None]
    grad_hi, grad_lo = split_table(node_columns(gradient_table))
    force_hi, force_lo = split_table(node_columns(weighted_table).T)
    inter_hi, inter_lo = split_table(interpolate.astype(np.float32))
    proj_hi, proj_lo = split_table(projection.astype(np.float32))
    return (
        jnp.asarray(np.concatenate([grad_hi, grad_hi, grad_lo], 1)),
        jnp.asarray(np.concatenate([force_hi, force_lo], 0)),
        jnp.asarray(np.concatenate([inter_hi, inter_lo], 1)),
        jnp.asarray(np.concatenate([proj_hi, proj_lo], 0)),
    )


def split_two(values):
    high = values.astype(BF16)
    return (high, (values - high.astype(F32)).astype(BF16))


def split_three(values):
    high = values.astype(BF16)
    rest = values - high.astype(F32)
    middle = rest.astype(BF16)
    return (high, middle, (rest - middle.astype(F32)).astype(BF16))


def mm(left, right, dims=((1,), (0,))):
    return lax.dot_general(left, right, (dims, ((), ())), preferred_element_type=F32)


def iota(shape, axis):
    return lax.broadcasted_iota(jnp.int32, shape, axis)


def line_selector(to_zones):
    lattice = iota((512, 512), 0 if to_zones else 1)
    grouped = iota((512, 512), 1 if to_zones else 0)
    return jnp.where(4 * (grouped % 128) + grouped // 128 == lattice, 1.0, 0.0).astype(BF16)


def mode_columns():
    row = iota((2 * MODES, WIDTH), 0)
    column = iota((2 * MODES, WIDTH), 1)
    return jnp.where(FIELDS * (row % MODES) + row // MODES == column, 1.0, 0.0).astype(BF16)


def pick_modes(fields):
    return mm(mode_columns(), fields, ((1,), (1,)))


def zone_math(velocity_of, modes, grad_ref, force_ref, inter_ref, proj_ref, nodes_ref, high_ref, low_ref,
              rate_high_ref, rate_low_ref, lattice_ref, face_up_ref, edge_up_ref, face_down_ref, edge_down_ref, modes_ref):
    zones = ZONE_COUNT
    for comp in range(3):
        line = velocity_of(comp)
        lanes = slice(zones * comp, zones * (comp + 1))
        groups = [line[:, zones * u : zones * (u + 1)] for u in range(4)]
        groups.append(pltpu.roll(groups[0], zones - 1, 1))
        for u in range(5):
            high, low = split_two(groups[u])
            nodes_ref[ROWS * u : ROWS * (u + 1), lanes] = high
            nodes_ref[ROWS * (5 + u) : ROWS * (6 + u), lanes] = low
            nodes_ref[ROWS * (10 + u) : ROWS * (11 + u), lanes] = high
    both = jnp.concatenate([modes[:MODES], modes[MODES:]], 1)
    twice = jnp.concatenate([both, both], 0).astype(BF16)
    chunk = 128
    for part in range(POINTS // chunk):
        rows = slice(chunk * part, chunk * (part + 1))
        nodes = nodes_ref[...]
        grads = []
        for first in range(3):
            start = POINTS * first + chunk * part
            flat = mm(grad_ref[start : start + chunk, :], nodes)
            grads.append([flat[:, zones * c : zones * (c + 1)] for c in range(3)])
        points = mm(inter_ref[rows, :], twice)
        rho = points[:, :zones]
        energy = points[:, zones:]
        divergence = grads[0][0] + grads[1][1] + grads[2][2]
        pressure = GAMMA_LESS * energy
        viscous = 0.5 * VISCOSITY * rho
        heating = None
        for first in range(3):
            for second in range(first, 3):
                total = grads[first][second] + grads[second][first]
                entry = viscous * total
                if first == second:
                    entry = entry - pressure
                    work = entry * grads[first][first]
                else:
                    work = entry * total
                heating = work if heating is None else heating + work
                high, low = split_two(entry)
                for d, c in ((first, second), (second, first))[: 1 if first == second else 2]:
                    at = slice(POINTS * d + chunk * part, POINTS * d + chunk * (part + 1))
                    lanes = slice(zones * c, zones * (c + 1))
                    high_ref[at, lanes] = high
                    low_ref[at, lanes] = low
        for column, rate in ((0, -rho * divergence), (zones, heating - energy * divergence)):
            high, low = split_two(rate)
            rate_high_ref[rows, column : column + zones] = high
            rate_low_ref[rows, column : column + zones] = low
    nodal = 5 * ROWS
    main = mm(force_ref[...], high_ref[...])
    force = main[:nodal] + main[nodal:] + mm(force_ref[:nodal, :], low_ref[...])
    for comp in range(3):
        lanes = slice(zones * comp, zones * (comp + 1))
        for u in range(4):
            block = force[ROWS * u : ROWS * (u + 1), lanes]
            if u == 0:
                block = block + pltpu.roll(force[ROWS * 4 : ROWS * 5, lanes], 1, 1)
            lattice_ref[comp, :, zones * u : zones * (u + 1)] = block
    for comp in range(3):
        for s in range(5):
            face_up_ref[5 * comp + s, :] = lattice_ref[comp, 5 * s + 4, :]
            if face_down_ref is not None:
                face_down_ref[5 * comp + s, :] = lattice_ref[comp, 5 * s, :]
        edge_up_ref[5 * comp : 5 * comp + 5, :] = lattice_ref[comp, 20:25, :]
        if edge_down_ref is not None:
            edge_down_ref[5 * comp : 5 * comp + 5, :] = lattice_ref[comp, 0:5, :]
    main = mm(proj_ref[...], rate_high_ref[...])
    change = main[:MODES] + main[MODES:] + mm(proj_ref[:MODES, :], rate_low_ref[...])
    both = both + TIME_STEP * change
    modes_ref[:MODES, :] = both[:, :zones].astype(BF16)
    modes_ref[MODES:, :] = both[:, zones:].astype(BF16)


def zone_first_kernel(velocity_ref, mass_ref, halo_a_ref, halo_b_ref, halo_c_ref, fields_hbm, grad_hbm, force_hbm,
                      inter_hbm, proj_hbm, state_ref, lattice_ref, up_ref, edge_up_ref, down_ref, edge_down_ref, modes_ref,
                      native_ref, fields_ref, grad_ref, force_ref, inter_ref, proj_ref, sems, *scratch):
    copies = fetch(
        (fields_hbm, grad_hbm, force_hbm, inter_hbm, proj_hbm),
        (fields_ref, grad_ref, force_ref, inter_ref, proj_ref),
        sems,
    )
    for comp in range(4):
        base = ROWS * comp
        native_ref[base + 24 : base + 32, :] = jnp.full((8, LINE), 1.0 if comp == 3 else 0.0, F32)
        for s in range(4):
            own = mass_ref[s] if comp == 3 else velocity_ref[comp, s]
            native_ref[base + 5 * s : base + 5 * s + 4, :] = own
            native_ref[base + 5 * s + 4, :] = halo_b_ref[comp, s, :]
        native_ref[base + 20 : base + 24, :] = halo_a_ref[comp]
        native_ref[base + 24, :] = halo_c_ref[comp, 0, :]
    selector = line_selector(True)
    count = 4 * ROWS
    for half in range(2):
        pieces = jnp.concatenate(split_three(native_ref[:, 512 * half : 512 * (half + 1)]), 0)
        moved = mm(pieces, selector)
        moved = moved[:count] + moved[count : 2 * count] + moved[2 * count :]
        for comp in range(4):
            for u in range(4):
                lanes = slice(256 * u + 128 * half, 256 * u + 128 * (half + 1))
                state_ref[comp, :, lanes] = moved[ROWS * comp : ROWS * (comp + 1), 128 * u : 128 * (u + 1)]
    copies[0].wait()
    modes = pick_modes(fields_ref[...])
    for copy in copies[1:]:
        copy.wait()
    zone_math(lambda comp: state_ref[comp], modes, grad_ref, force_ref, inter_ref, proj_ref, *scratch,
              lattice_ref, up_ref, edge_up_ref, down_ref, edge_down_ref, modes_ref)


def add_faces(total_ref, low_ref, upper_ref):
    for comp in range(3):
        for s in range(5):
            at = 5 * comp + s
            total_ref[comp, 5 * s, :] = total_ref[comp, 5 * s, :] + low_ref[at, :]
            if upper_ref is not None:
                total_ref[comp, 5 * s + 4, :] = total_ref[comp, 5 * s + 4, :] + upper_ref[at, :]


def join_edge(block_ref):
    pair = block_ref[CAPACITY:FOLDED, :WIDTH].astype(F32)
    return pair[:, :LINE] + pair[:, LINE:]


def zone_second_kernel(state_ref, first_ref, low_ref, upper_ref, middle_ref, in_low_ref, in_upper_ref, grad_ref,
                       force_ref, inter_ref, proj_ref, fields_ref, total_ref, lattice_ref, up_ref, edge_up_ref,
                       modes_ref, edge_ref, *scratch):
    fields = sum_slots(middle_ref, in_low_ref, in_upper_ref)
    fields_ref[...] = fields
    total_ref[...] = first_ref[...]
    add_faces(total_ref, low_ref, upper_ref)
    for row, block_ref in ((0, in_low_ref), (20, in_upper_ref)):
        edge_ref[...] = join_edge(block_ref)
        for comp in range(3):
            at = slice(5 * comp, 5 * comp + 5)
            total_ref[comp, row : row + 5, :] = total_ref[comp, row : row + 5, :] + edge_ref[at, :]
    factor = TIME_STEP / state_ref[3]
    modes = pick_modes(fields)
    zone_math(lambda comp: state_ref[comp] - total_ref[comp] * factor, modes, grad_ref, force_ref, inter_ref,
              proj_ref, *scratch, lattice_ref, up_ref, edge_up_ref, None, None, modes_ref)


def sum_slots(*block_refs):
    incoming = jnp.concatenate([ref[:CAPACITY, :] for ref in block_refs], 0)
    codes = incoming[:, WIDTH:].astype(F32)
    label = iota((SLOTS, 128), 1).astype(F32)
    chosen = [jnp.where(codes == label + 128.0 * half, 1.0, 0.0).astype(BF16) for half in range(ZONE_COUNT // 128)]
    selector = jnp.concatenate(chosen, 1)
    return mm(selector, incoming[:, :WIDTH], ((0,), (0,))).astype(BF16)


def remap_kernel(step, blocks, fields_ref, modes_ref, source_ref, target_ref, *refs):
    number = len(blocks)
    matrix_refs, outs = refs[:number], refs[number : 2 * number]
    picked_ref, result_ref = refs[2 * number :]
    slots = CAPACITY * number

    def slots_of(ref):
        pieces = [ref[step : step + 1, CAPACITY * block : CAPACITY * (block + 1)] for block in blocks]
        return pieces[0] if number == 1 else jnp.concatenate(pieces, 1)

    zone = iota((ZONE_COUNT, slots), 0)
    chosen = jnp.where(zone == slots_of(source_ref), 1.0, 0.0).astype(BF16)
    picked = mm(chosen, fields_ref[...], ((0,), (0,)))
    new = mm(chosen, modes_ref[...].T, ((0,), (0,))).astype(BF16)
    new = mm(new, mode_columns())
    lane = iota((slots, 128), 1)
    group = lane // FIELDS
    renewed = lane % FIELDS < 2
    for g in range(WIDTH // 128):
        lanes = slice(128 * g, 128 * (g + 1))
        piece = jnp.where(renewed, new[:, lanes], picked[:, lanes])
        for r in range(4):
            picked_ref[pl.ds(4 * g + r, slots, stride=MODES), :] = jnp.where(group == r, piece, 0.0)
    for place, matrix_ref in enumerate(matrix_refs):

        def multiply(trip, carry):
            for inner in range(16):
                slot = 16 * trip + inner
                at = pl.ds(pl.multiple_of(MODES * (CAPACITY * place + slot), MODES), MODES)
                result_ref[at, :] = mm(matrix_ref[0, slot], picked_ref[at, :].astype(BF16))
            return carry

        lax.fori_loop(0, CAPACITY // 16, multiply, 0)
    for g in range(WIDTH // 128):
        rows = [result_ref[pl.ds(4 * g + r, slots, stride=MODES), :] for r in range(4)]
        total = None
        for shift in range(4):
            mixed = rows[3]
            for r in range(3):
                mixed = jnp.where(group == (r + shift) % 4, rows[r], mixed)
            if shift:
                mixed = pltpu.roll(mixed, 128 - FIELDS * shift, 1)
            total = mixed if total is None else total + mixed
        total = total.astype(BF16)
        for place in range(number):
            outs[place][:, 128 * g : 128 * (g + 1)] = total[CAPACITY * place : CAPACITY * (place + 1)]
    codes = jnp.broadcast_to(slots_of(target_ref).astype(F32), (8, slots))
    codes = jnp.where(iota((8, slots), 0) == 0, codes, 0.0).astype(BF16)
    codes = mm(codes, jnp.ones((8, 128), BF16), ((0,), (0,))).astype(BF16)
    for place in range(number):
        outs[place][:, WIDTH:] = codes[CAPACITY * place : CAPACITY * (place + 1)]


def fold_edge(edge_ref, source_row, low_ref, upper_ref, stage_ref, out_ref):
    stage_ref[15:16, :] = jnp.zeros((1, LINE), F32)
    stage_ref[0:15, :] = edge_ref[...]
    for comp in range(3):
        at = 5 * comp
        stage_ref[at, :] = stage_ref[at, :] + low_ref[at + source_row, :]
        if upper_ref is not None:
            stage_ref[at + 4, :] = stage_ref[at + 4, :] + upper_ref[at + source_row, :]
    high, low = split_two(stage_ref[...])
    out_ref[:, :LINE] = high
    out_ref[:, LINE:WIDTH] = low
    out_ref[:, WIDTH:] = jnp.zeros((16, 128), BF16)


def fold_kernel(source_row, block_any, edge_ref, *refs):
    upper_ref = refs[1] if len(refs) == 4 else None
    fold_edge(edge_ref, source_row, refs[0], upper_ref, refs[-1], refs[-2])


def interleave(stage_ref, force_ref):
    count = stage_ref.shape[0]
    selector = line_selector(False)
    for half in range(2):
        grouped = jnp.concatenate(
            [stage_ref[:, 256 * u + 128 * half : 256 * u + 128 * (half + 1)] for u in range(4)], 1
        )
        moved = mm(jnp.concatenate(split_two(grouped), 0), selector)
        force_ref[:, 512 * half : 512 * (half + 1)] = moved[:count] + moved[count:]


def update_kernel(velocity_ref, displacement_ref, mass_ref, first_ref, second_ref, low_ref, velocity_out_ref,
                  displacement_out_ref, stage_ref, force_ref):
    for comp in range(3):
        for s in range(4):
            at = 16 * comp + 4 * s
            stage_ref[at : at + 4, :] = first_ref[comp, 5 * s : 5 * s + 4, :]
            stage_ref[48 + at : 48 + at + 4, :] = second_ref[comp, 5 * s : 5 * s + 4, :]
            stage_ref[48 + at, :] = stage_ref[48 + at, :] + low_ref[5 * comp + s, :]
    interleave(stage_ref, force_ref)
    for s in range(4):
        factor = TIME_STEP / mass_ref[s]
        for comp in range(3):
            at = 16 * comp + 4 * s
            middle = velocity_ref[comp, s] - force_ref[at : at + 4, :] * factor
            last = middle - force_ref[48 + at : 48 + at + 4, :] * factor
            velocity_out_ref[comp, s] = last
            displacement_out_ref[comp, s] = displacement_ref[comp, s] + TIME_STEP * middle + TIME_STEP * last


def finish_kernel(velocity_ref, displacement_ref, mass_ref, middle_ref, in_low_ref, in_upper_ref, fields_ref,
                  velocity_out_ref, displacement_out_ref, stage_ref, force_ref):
    fields_ref[...] = sum_slots(middle_ref, in_low_ref, in_upper_ref)
    stage_ref[...] = join_edge(in_low_ref)
    interleave(stage_ref, force_ref)
    factor = TIME_STEP / mass_ref[0]
    for comp in range(3):
        change = force_ref[5 * comp : 5 * comp + 4, :] * factor
        velocity_out_ref[comp, 0] = velocity_ref[comp, 0] - change
        displacement_out_ref[comp, 0] = displacement_ref[comp, 0] - TIME_STEP * change


def fetch(sources, targets, sems):
    copies = [pltpu.make_async_copy(a, b, sems.at[i]) for i, (a, b) in enumerate(zip(sources, targets))]
    for copy in copies:
        copy.start()
    return copies


def pack_kernel(velocity_hbm, mass_hbm, send_a_ref, send_b_ref, send_c_ref, velocity_ref, mass_ref, sems):
    for copy in fetch((velocity_hbm, mass_hbm), (velocity_ref, mass_ref), sems):
        copy.wait()
    for comp in range(4):
        for s in range(4):
            own = mass_ref[s] if comp == 3 else velocity_ref[comp, s]
            if s == 0:
                send_a_ref[comp] = own
                send_c_ref[comp] = own[:1]
            send_b_ref[comp, s : s + 1, :] = own[:1]


def shape(*dims, dtype=F32):
    return jax.ShapeDtypeStruct(dims, dtype)


LATTICE = (3, ROWS, LINE)
FACE = (15, LINE)


def zone_scratch():
    return [
        pltpu.VMEM((15 * ROWS, 3 * ZONE_COUNT), BF16),
        pltpu.VMEM((3 * POINTS, 3 * ZONE_COUNT), BF16),
        pltpu.VMEM((3 * POINTS, 3 * ZONE_COUNT), BF16),
        pltpu.VMEM((POINTS, 2 * ZONE_COUNT), BF16),
        pltpu.VMEM((POINTS, 2 * ZONE_COUNT), BF16),
    ]


def whole(*dims):
    return pl.BlockSpec(dims, lambda i: (0,) * len(dims))


def cost(microseconds):
    return pl.CostEstimate(flops=int(microseconds * 1e9), bytes_accessed=int(microseconds * 3e6), transcendentals=0)


LIMIT = pltpu.CompilerParams(vmem_limit_bytes=40 * 1024 * 1024)
FAR = pl.BlockSpec(memory_space=pltpu.HBM)
ANYWHERE = pl.BlockSpec(memory_space=pl.ANY)
EDGE_BLOCK = pl.BlockSpec((16, SENT), lambda i: (CAPACITY // 16, 0))


def remap_call(step, blocks, rows, fields, modes, matrix, source, target):
    return pl.pallas_call(
        lambda *refs: remap_kernel(step, blocks, *refs),
        grid=(1,),
        in_specs=[whole(ZONE_COUNT, WIDTH), whole(2 * MODES, ZONE_COUNT), whole(STEPS, SLOTS), whole(STEPS, SLOTS)]
        + [pl.BlockSpec((1, CAPACITY, MODES, MODES), lambda i, block=block: (0, block, 0, 0)) for block in blocks],
        out_specs=[whole(CAPACITY, SENT)] * len(blocks),
        out_shape=[shape(count, SENT, dtype=BF16) for count in rows],
        scratch_shapes=[pltpu.VMEM((CAPACITY * len(blocks) * MODES, 128), F32)] * 2,
        compiler_params=LIMIT,
        cost_estimate=cost(0.7),
        name="remap_step",
    )(fields, modes, source, target, *[matrix] * len(blocks))


def far(*arrays):
    return [pltpu.with_memory_space_constraint(array, pltpu.HBM) for array in arrays]


def fold_call(source_row, block, edge, *faces):
    return pl.pallas_call(
        lambda *refs: fold_kernel(source_row, *refs),
        grid=(1,),
        in_specs=[ANYWHERE] + [whole(*FACE)] * (1 + len(faces)),
        out_specs=EDGE_BLOCK,
        out_shape=shape(FOLDED, SENT, dtype=BF16),
        input_output_aliases={0: 0},
        scratch_shapes=[pltpu.VMEM((16, LINE), F32)],
        compiler_params=LIMIT,
        cost_estimate=cost(0.5),
        name="fold_edges",
    )(block, edge, *near(*faces))


def near(*arrays):
    return [pltpu.with_memory_space_constraint(array, pltpu.VMEM) for array in arrays]


def body(fields, velocity, displacement, node_mass, remap_matrix, remap_source, remap_target):
    tables = basis_tables()
    lines = ("gx", "gy")
    send_a, send_b, send_c = pl.pallas_call(
        pack_kernel,
        in_specs=[FAR] * 2,
        out_shape=[shape(4, 4, LINE), shape(4, 4, LINE), shape(4, 1, LINE)],
        scratch_shapes=[
            pltpu.VMEM((3, 4, 4, LINE), F32),
            pltpu.VMEM((4, 4, LINE), F32),
            pltpu.SemaphoreType.DMA((2,)),
        ],
        compiler_params=LIMIT,
        cost_estimate=cost(1),
        name="pack_halo",
    )(*far(velocity, node_mass))
    size_a = lax.axis_size(lines)
    size_b = lax.axis_size("gz")
    corner = [
        (((i + 1) % size_a) * size_b + (j + 1) % size_b, i * size_b + j)
        for i in range(size_a)
        for j in range(size_b)
    ]
    halo_a = from_behind(send_a, lines, -1)
    halo_b = from_behind(send_b, "gz", -1)
    halo_c = lax.ppermute(send_c, ("gx", "gy", "gz"), corner)
    lattice = shape(*LATTICE)
    face = shape(*FACE)
    modes_shape = shape(2 * MODES, ZONE_COUNT, dtype=BF16)
    folded = shape(FOLDED, SENT, dtype=BF16)
    state, partial, up, edge_up, down, edge_down, modes = pl.pallas_call(
        zone_first_kernel,
        in_specs=[pl.BlockSpec(memory_space=pltpu.VMEM)] * 5 + [FAR] * 5,
        out_shape=[shape(4, ROWS, LINE), lattice, face, face, face, face, modes_shape],
        scratch_shapes=[pltpu.VMEM((4 * ROWS, LINE), F32)]
        + [pltpu.VMEM(array.shape, array.dtype) for array in (fields,) + tables]
        + [pltpu.SemaphoreType.DMA((5,))]
        + zone_scratch(),
        compiler_params=LIMIT,
        cost_estimate=cost(7),
        name="zone_first",
    )(velocity, node_mass, *near(halo_a, halo_b, halo_c), *far(fields, *tables))
    from_low = from_behind(up, "gz", 1)
    from_up = from_behind(down, "gz", -1)
    index = (remap_source, remap_target)
    matrix = remap_matrix[0:1]
    matrix_late = remap_matrix[1:2]
    (upper,) = remap_call(0, (2,), (FOLDED,), fields, modes, matrix, *index)
    upper = fold_call(4, upper, edge_up, from_low, from_up)
    fields, modes, upper = lax.optimization_barrier((fields, modes, upper))
    in_low = from_behind(upper, lines, 1)
    (low,) = remap_call(0, (0,), (FOLDED,), fields, modes, matrix, *index)
    low = fold_call(0, low, edge_down, from_low, from_up)
    fields, modes, low, matrix_late = lax.optimization_barrier((fields, modes, low, matrix_late))
    in_upper = from_behind(low, lines, -1)
    (middle,) = remap_call(0, (1,), (CAPACITY,), fields, modes, matrix, *index)
    fields, first, partial, up, edge_up, modes = pl.pallas_call(
        zone_second_kernel,
        out_shape=[shape(ZONE_COUNT, WIDTH, dtype=BF16), lattice, lattice, face, face, modes_shape],
        scratch_shapes=[pltpu.VMEM((16, LINE), F32)] + zone_scratch(),
        compiler_params=LIMIT,
        cost_estimate=cost(7),
        name="zone_second",
    )(state, partial, *near(from_low, from_up), middle, *near(in_low, in_upper, *tables))
    from_low = from_behind(up, "gz", 1)
    matrix = matrix_late
    (low,) = remap_call(1, (0,), (CAPACITY,), fields, modes, matrix, *index)
    fields, modes, low = lax.optimization_barrier((fields, modes, low))
    in_upper = from_behind(low, lines, -1)
    (upper,) = remap_call(1, (2,), (FOLDED,), fields, modes, matrix, *index)
    upper = fold_call(4, upper, edge_up, from_low)
    fields, modes, upper = lax.optimization_barrier((fields, modes, upper))
    in_low = from_behind(upper, lines, 1)
    (middle,) = remap_call(1, (1,), (CAPACITY,), fields, modes, matrix, *index)
    nodal = shape(*velocity.shape)
    velocity_part, displacement_part = pl.pallas_call(
        update_kernel,
        out_shape=[nodal, nodal],
        scratch_shapes=[pltpu.VMEM((96, LINE), F32)] * 2,
        compiler_params=LIMIT,
        cost_estimate=cost(2.5),
        name="update_nodes",
    )(velocity, displacement, node_mass, first, partial, *near(from_low))
    bottom = whole(3, 1, 4, LINE)
    fields_out, velocity_out, displacement_out = pl.pallas_call(
        finish_kernel,
        grid=(1,),
        in_specs=[
            bottom,
            bottom,
            whole(1, 4, LINE),
            whole(CAPACITY, SENT),
            whole(FOLDED, SENT),
            whole(CAPACITY, SENT),
        ],
        out_specs=[whole(ZONE_COUNT, WIDTH), bottom, bottom],
        out_shape=[shape(ZONE_COUNT, WIDTH, dtype=BF16), nodal, nodal],
        input_output_aliases={0: 1, 1: 2},
        scratch_shapes=[pltpu.VMEM((16, LINE), F32)] * 2,
        compiler_params=LIMIT,
        cost_estimate=cost(3),
        name="finish_step",
    )(velocity_part, displacement_part, node_mass, middle, *near(in_low, in_upper))
    return (fields_out, velocity_out, displacement_out)


def solution(mesh):
    in_specs = (
        P(("gx", "gy", "gz"), None),
        P(None, ("gx", "gy"), "gz", None),
        P(None, ("gx", "gy"), "gz", None),
        P(("gx", "gy"), "gz", None),
        P(None, ("gx", "gy", "gz"), None, None),
        P(None, ("gx", "gy", "gz")),
        P(None, ("gx", "gy", "gz")),
    )
    out_specs = (
        P(("gx", "gy", "gz"), None),
        P(None, ("gx", "gy"), "gz", None),
        P(None, ("gx", "gy"), "gz", None),
    )
    return jax.shard_map(body, mesh=mesh, in_specs=in_specs, out_specs=out_specs, check_vma=False)
```

```python
import math

import jax
import jax.numpy as jnp
import numpy as np
from jax import lax
from jax.experimental import pallas as pl
from jax.experimental.layout import Layout, with_layout_constraint
from jax.experimental.pallas import tpu as pltpu
from jax.sharding import PartitionSpec as P

NODES = 125
POINTS = 512
MODES = 64
FIELDS = 32
STEPS = 2


TIME_STEP = 0.3
GAMMA_LESS = 0.4
VISCOSITY = 0.3
F32 = jnp.float32
BF16 = jnp.bfloat16
ZONE_COUNT = 256
ROWS = 32
LINE = 1024
CAPACITY = 32
SLOTS = 96
WIDTH = MODES * FIELDS
SENT = WIDTH + 128
FOLDED = CAPACITY + 16


def from_behind(shard, axis, by):
    size = lax.axis_size(axis)
    return lax.ppermute(shard, axis, [(i, (i + by) % size) for i in range(size)])


def gauss_rule(order):
    if order == 8:
        half_points = [
            0.1834346424956498,
            0.525532409916329,
            0.7966664774136267,
            0.9602898564975363,
        ]
        half_weights = [
            0.362683783378362,
            0.3137066458778873,
            0.2223810344533745,
            0.1012285362903763,
        ]
    else:
        half_points = [0.3399810435848563, 0.8611363115940526]
        half_weights = [0.6521451548625461, 0.3478548451374538]
    points = np.array([-value for value in half_points[::-1]] + half_points)
    weights = np.array(half_weights[::-1] + half_weights)
    return (points, weights)


def lagrange_tables(nodes, points):
    values = np.ones((points.shape[0], nodes.shape[0]))
    slopes = np.zeros((points.shape[0], nodes.shape[0]))
    for column in range(nodes.shape[0]):
        for other in range(nodes.shape[0]):
            if other != column:
                values[:, column] *= (points - nodes[other]) / (nodes[column] - nodes[other])
        for other in range(nodes.shape[0]):
            if other != column:
                product = np.ones(points.shape) / (nodes[column] - nodes[other])
                for third in range(nodes.shape[0]):
                    if third != column and third != other:
                        product = product * (points - nodes[third]) / (nodes[column] - nodes[third])
                slopes[:, column] += product
    return (values, slopes)


def kron_three(first, second, third):
    return np.kron(np.kron(first, second), third)


def split_table(table):
    high = table.astype(jnp.bfloat16)
    low = (table - high.astype(np.float32)).astype(jnp.bfloat16)
    return (high, low)


def node_columns(table):
    grid = table.reshape(-1, 5, 25 // 5, 5).transpose(0, 3, 1, 2).reshape(-1, 5, 25)
    return np.pad(grid, ((0, 0), (0, 0), (0, ROWS - 25))).reshape(-1, 5 * ROWS)


def basis_tables():
    gauss_points, gauss_weights = gauss_rule(8)
    points = (gauss_points + 1.0) / 2.0
    weights = gauss_weights / 2.0
    root = math.sqrt(3.0 / 7.0)
    lobatto = (np.array([-1.0, -root, 0.0, root, 1.0]) + 1.0) / 2.0
    four_points, four_weights = gauss_rule(4)
    legendre_nodes = (four_points + 1.0) / 2.0
    node_values, node_slopes = lagrange_tables(lobatto, points)
    mode_values, unused_slopes = lagrange_tables(legendre_nodes, points)
    gradient_table = np.concatenate(
        [
            kron_three(node_slopes, node_values, node_values),
            kron_three(node_values, node_slopes, node_values),
            kron_three(node_values, node_values, node_slopes),
        ],
        0,
    )
    interpolate = kron_three(mode_values, mode_values, mode_values)
    weight_table = kron_three(weights, weights, weights)
    mass_diagonal = four_weights / 2.0
    project_line = mode_values.T * weights[None, :] / mass_diagonal[:, None]
    projection = kron_three(project_line, project_line, project_line)
    gradient_table = gradient_table.astype(np.float32)
    weighted_table = gradient_table * np.tile(weight_table.astype(np.float32), 3)[:, None]
    grad_hi, grad_lo = split_table(node_columns(gradient_table))
    force_hi, force_lo = split_table(node_columns(weighted_table).T)
    inter_hi, inter_lo = split_table(interpolate.astype(np.float32))
    proj_hi, proj_lo = split_table(projection.astype(np.float32))
    return (
        jnp.asarray(np.concatenate([grad_hi, grad_hi, grad_lo], 1)),
        jnp.asarray(np.concatenate([force_hi, force_lo], 0)),
        jnp.asarray(np.concatenate([inter_hi, inter_lo], 1)),
        jnp.asarray(np.concatenate([proj_hi, proj_lo], 0)),
    )


def split_two(values):
    high = values.astype(BF16)
    return (high, (values - high.astype(F32)).astype(BF16))


def split_three(values):
    high = values.astype(BF16)
    rest = values - high.astype(F32)
    middle = rest.astype(BF16)
    return (high, middle, (rest - middle.astype(F32)).astype(BF16))


def mm(left, right, dims=((1,), (0,))):
    return lax.dot_general(left, right, (dims, ((), ())), preferred_element_type=F32)


def iota(shape, axis):
    return lax.broadcasted_iota(jnp.int32, shape, axis)


def line_selector(to_zones):
    lattice = iota((512, 512), 0 if to_zones else 1)
    grouped = iota((512, 512), 1 if to_zones else 0)
    return jnp.where(4 * (grouped % 128) + grouped // 128 == lattice, 1.0, 0.0).astype(BF16)


def mode_columns():
    row = iota((2 * MODES, WIDTH), 0)
    column = iota((2 * MODES, WIDTH), 1)
    return jnp.where(FIELDS * (row % MODES) + row // MODES == column, 1.0, 0.0).astype(BF16)


def pick_modes(fields):
    return mm(mode_columns(), fields, ((1,), (1,)))


def zone_math(velocity_of, modes, grad_ref, force_ref, inter_ref, proj_ref, nodes_ref, high_ref, low_ref,
              rate_high_ref, rate_low_ref, lattice_ref, face_up_ref, edge_up_ref, face_down_ref, edge_down_ref, modes_ref):
    zones = ZONE_COUNT
    for comp in range(3):
        line = velocity_of(comp)
        lanes = slice(zones * comp, zones * (comp + 1))
        groups = [line[:, zones * u : zones * (u + 1)] for u in range(4)]
        groups.append(pltpu.roll(groups[0], zones - 1, 1))
        for u in range(5):
            high, low = split_two(groups[u])
            nodes_ref[ROWS * u : ROWS * (u + 1), lanes] = high
            nodes_ref[ROWS * (5 + u) : ROWS * (6 + u), lanes] = low
            nodes_ref[ROWS * (10 + u) : ROWS * (11 + u), lanes] = high
    both = jnp.concatenate([modes[:MODES], modes[MODES:]], 1)
    twice = jnp.concatenate([both, both], 0).astype(BF16)
    chunk = 128
    for part in range(POINTS // chunk):
        rows = slice(chunk * part, chunk * (part + 1))
        nodes = nodes_ref[...]
        grads = []
        for first in range(3):
            start = POINTS * first + chunk * part
            flat = mm(grad_ref[start : start + chunk, :], nodes)
            grads.append([flat[:, zones * c : zones * (c + 1)] for c in range(3)])
        points = mm(inter_ref[rows, :], twice)
        rho = points[:, :zones]
        energy = points[:, zones:]
        divergence = grads[0][0] + grads[1][1] + grads[2][2]
        pressure = GAMMA_LESS * energy
        viscous = 0.5 * VISCOSITY * rho
        heating = None
        for first in range(3):
            for second in range(first, 3):
                total = grads[first][second] + grads[second][first]
                entry = viscous * total
                if first == second:
                    entry = entry - pressure
                    work = entry * grads[first][first]
                else:
                    work = entry * total
                heating = work if heating is None else heating + work
                high, low = split_two(entry)
                for d, c in ((first, second), (second, first))[: 1 if first == second else 2]:
                    at = slice(POINTS * d + chunk * part, POINTS * d + chunk * (part + 1))
                    lanes = slice(zones * c, zones * (c + 1))
                    high_ref[at, lanes] = high
                    low_ref[at, lanes] = low
        for column, rate in ((0, -rho * divergence), (zones, heating - energy * divergence)):
            high, low = split_two(rate)
            rate_high_ref[rows, column : column + zones] = high
            rate_low_ref[rows, column : column + zones] = low
    nodal = 5 * ROWS
    main = mm(force_ref[...], high_ref[...])
    force = main[:nodal] + main[nodal:] + mm(force_ref[:nodal, :], low_ref[...])
    for comp in range(3):
        lanes = slice(zones * comp, zones * (comp + 1))
        for u in range(4):
            block = force[ROWS * u : ROWS * (u + 1), lanes]
            if u == 0:
                block = block + pltpu.roll(force[ROWS * 4 : ROWS * 5, lanes], 1, 1)
            lattice_ref[comp, :, zones * u : zones * (u + 1)] = block
    for comp in range(3):
        for s in range(5):
            face_up_ref[5 * comp + s, :] = lattice_ref[comp, 5 * s + 4, :]
            if face_down_ref is not None:
                face_down_ref[5 * comp + s, :] = lattice_ref[comp, 5 * s, :]
        edge_up_ref[5 * comp : 5 * comp + 5, :] = lattice_ref[comp, 20:25, :]
        if edge_down_ref is not None:
            edge_down_ref[5 * comp : 5 * comp + 5, :] = lattice_ref[comp, 0:5, :]
    main = mm(proj_ref[...], rate_high_ref[...])
    change = main[:MODES] + main[MODES:] + mm(proj_ref[:MODES, :], rate_low_ref[...])
    both = both + TIME_STEP * change
    modes_ref[:MODES, :] = both[:, :zones].astype(BF16)
    modes_ref[MODES:, :] = both[:, zones:].astype(BF16)


def zone_first_kernel(velocity_ref, mass_ref, halo_a_ref, halo_b_ref, halo_c_ref, fields_hbm, grad_hbm, force_hbm,
                      inter_hbm, proj_hbm, state_ref, lattice_ref, up_ref, edge_up_ref, down_ref, edge_down_ref, modes_ref,
                      native_ref, fields_ref, grad_ref, force_ref, inter_ref, proj_ref, sems, *scratch):
    copies = fetch(
        (fields_hbm, grad_hbm, force_hbm, inter_hbm, proj_hbm),
        (fields_ref, grad_ref, force_ref, inter_ref, proj_ref),
        sems,
    )
    for comp in range(4):
        base = ROWS * comp
        native_ref[base + 24 : base + 32, :] = jnp.full((8, LINE), 1.0 if comp == 3 else 0.0, F32)
        for s in range(4):
            own = mass_ref[s] if comp == 3 else velocity_ref[comp, s]
            native_ref[base + 5 * s : base + 5 * s + 4, :] = own
            native_ref[base + 5 * s + 4, :] = halo_b_ref[comp, s, :]
        native_ref[base + 20 : base + 24, :] = halo_a_ref[comp]
        native_ref[base + 24, :] = halo_c_ref[comp, 0, :]
    selector = line_selector(True)
    count = 4 * ROWS
    for half in range(2):
        pieces = jnp.concatenate(split_three(native_ref[:, 512 * half : 512 * (half + 1)]), 0)
        moved = mm(pieces, selector)
        moved = moved[:count] + moved[count : 2 * count] + moved[2 * count :]
        for comp in range(4):
            for u in range(4):
                lanes = slice(256 * u + 128 * half, 256 * u + 128 * (half + 1))
                state_ref[comp, :, lanes] = moved[ROWS * comp : ROWS * (comp + 1), 128 * u : 128 * (u + 1)]
    copies[0].wait()
    modes = pick_modes(fields_ref[...])
    for copy in copies[1:]:
        copy.wait()
    zone_math(lambda comp: state_ref[comp], modes, grad_ref, force_ref, inter_ref, proj_ref, *scratch,
              lattice_ref, up_ref, edge_up_ref, down_ref, edge_down_ref, modes_ref)


def add_faces(total_ref, low_ref, upper_ref):
    for comp in range(3):
        for s in range(5):
            at = 5 * comp + s
            total_ref[comp, 5 * s, :] = total_ref[comp, 5 * s, :] + low_ref[at, :]
            if upper_ref is not None:
                total_ref[comp, 5 * s + 4, :] = total_ref[comp, 5 * s + 4, :] + upper_ref[at, :]


def join_edge(block_ref):
    pair = block_ref[CAPACITY:FOLDED, :WIDTH].astype(F32)
    return pair[:, :LINE] + pair[:, LINE:]


def zone_second_kernel(state_ref, first_ref, low_ref, upper_ref, middle_ref, in_low_ref, in_upper_ref, grad_ref,
                       force_ref, inter_ref, proj_ref, fields_ref, total_ref, lattice_ref, up_ref, edge_up_ref,
                       modes_ref, edge_ref, *scratch):
    fields = sum_slots(middle_ref, in_low_ref, in_upper_ref)
    fields_ref[...] = fields
    total_ref[...] = first_ref[...]
    add_faces(total_ref, low_ref, upper_ref)
    for row, block_ref in ((0, in_low_ref), (20, in_upper_ref)):
        edge_ref[...] = join_edge(block_ref)
        for comp in range(3):
            at = slice(5 * comp, 5 * comp + 5)
            total_ref[comp, row : row + 5, :] = total_ref[comp, row : row + 5, :] + edge_ref[at, :]
    factor = TIME_STEP / state_ref[3]
    modes = pick_modes(fields)
    zone_math(lambda comp: state_ref[comp] - total_ref[comp] * factor, modes, grad_ref, force_ref, inter_ref,
              proj_ref, *scratch, lattice_ref, up_ref, edge_up_ref, None, None, modes_ref)


def sum_slots(*block_refs):
    incoming = jnp.concatenate([ref[:CAPACITY, :] for ref in block_refs], 0)
    codes = incoming[:, WIDTH:].astype(F32)
    label = iota((SLOTS, 128), 1).astype(F32)
    chosen = [jnp.where(codes == label + 128.0 * half, 1.0, 0.0).astype(BF16) for half in range(ZONE_COUNT // 128)]
    selector = jnp.concatenate(chosen, 1)
    return mm(selector, incoming[:, :WIDTH], ((0,), (0,))).astype(BF16)


def remap_kernel(step, blocks, fields_ref, modes_ref, source_ref, target_ref, *refs):
    number = len(blocks)
    matrix_refs, outs = refs[:number], refs[number : 2 * number]
    picked_ref, result_ref = refs[2 * number :]
    slots = CAPACITY * number

    def slots_of(ref):
        pieces = [ref[step : step + 1, CAPACITY * block : CAPACITY * (block + 1)] for block in blocks]
        return pieces[0] if number == 1 else jnp.concatenate(pieces, 1)

    zone = iota((ZONE_COUNT, slots), 0)
    chosen = jnp.where(zone == slots_of(source_ref), 1.0, 0.0).astype(BF16)
    picked = mm(chosen, fields_ref[...], ((0,), (0,)))
    new = mm(chosen, modes_ref[...].T, ((0,), (0,))).astype(BF16)
    new = mm(new, mode_columns())
    lane = iota((slots, 128), 1)
    group = lane // FIELDS
    renewed = lane % FIELDS < 2
    for g in range(WIDTH // 128):
        lanes = slice(128 * g, 128 * (g + 1))
        piece = jnp.where(renewed, new[:, lanes], picked[:, lanes])
        for r in range(4):
            picked_ref[pl.ds(4 * g + r, slots, stride=MODES), :] = jnp.where(group == r, piece, 0.0)
    for place, matrix_ref in enumerate(matrix_refs):

        def multiply(trip, carry):
            for inner in range(16):
                slot = 16 * trip + inner
                at = pl.ds(pl.multiple_of(MODES * (CAPACITY * place + slot), MODES), MODES)
                result_ref[at, :] = mm(matrix_ref[0, slot], picked_ref[at, :].astype(BF16))
            return carry

        lax.fori_loop(0, CAPACITY // 16, multiply, 0)
    for g in range(WIDTH // 128):
        rows = [result_ref[pl.ds(4 * g + r, slots, stride=MODES), :] for r in range(4)]
        total = None
        for shift in range(4):
            mixed = rows[3]
            for r in range(3):
                mixed = jnp.where(group == (r + shift) % 4, rows[r], mixed)
            if shift:
                mixed = pltpu.roll(mixed, 128 - FIELDS * shift, 1)
            total = mixed if total is None else total + mixed
        total = total.astype(BF16)
        for place in range(number):
            outs[place][:, 128 * g : 128 * (g + 1)] = total[CAPACITY * place : CAPACITY * (place + 1)]
    codes = jnp.broadcast_to(slots_of(target_ref).astype(F32), (8, slots))
    codes = jnp.where(iota((8, slots), 0) == 0, codes, 0.0).astype(BF16)
    codes = mm(codes, jnp.ones((8, 128), BF16), ((0,), (0,))).astype(BF16)
    for place in range(number):
        outs[place][:, WIDTH:] = codes[CAPACITY * place : CAPACITY * (place + 1)]


def fold_edge(edge_ref, source_row, low_ref, upper_ref, stage_ref, out_ref):
    stage_ref[15:16, :] = jnp.zeros((1, LINE), F32)
    stage_ref[0:15, :] = edge_ref[...]
    for comp in range(3):
        at = 5 * comp
        stage_ref[at, :] = stage_ref[at, :] + low_ref[at + source_row, :]
        if upper_ref is not None:
            stage_ref[at + 4, :] = stage_ref[at + 4, :] + upper_ref[at + source_row, :]
    high, low = split_two(stage_ref[...])
    out_ref[:, :LINE] = high
    out_ref[:, LINE:WIDTH] = low
    out_ref[:, WIDTH:] = jnp.zeros((16, 128), BF16)


def fold_kernel(source_row, block_any, edge_ref, *refs):
    upper_ref = refs[1] if len(refs) == 4 else None
    fold_edge(edge_ref, source_row, refs[0], upper_ref, refs[-1], refs[-2])


def interleave(stage_ref, force_ref):
    count = stage_ref.shape[0]
    selector = line_selector(False)
    for half in range(2):
        grouped = jnp.concatenate(
            [stage_ref[:, 256 * u + 128 * half : 256 * u + 128 * (half + 1)] for u in range(4)], 1
        )
        moved = mm(jnp.concatenate(split_two(grouped), 0), selector)
        force_ref[:, 512 * half : 512 * (half + 1)] = moved[:count] + moved[count:]


def update_kernel(velocity_ref, displacement_ref, mass_ref, first_ref, second_ref, low_ref, velocity_out_ref,
                  displacement_out_ref, stage_ref, force_ref):
    for comp in range(3):
        for s in range(4):
            at = 16 * comp + 4 * s
            stage_ref[at : at + 4, :] = first_ref[comp, 5 * s : 5 * s + 4, :]
            stage_ref[48 + at : 48 + at + 4, :] = second_ref[comp, 5 * s : 5 * s + 4, :]
            stage_ref[48 + at, :] = stage_ref[48 + at, :] + low_ref[5 * comp + s, :]
    interleave(stage_ref, force_ref)
    for s in range(4):
        factor = TIME_STEP / mass_ref[s]
        for comp in range(3):
            at = 16 * comp + 4 * s
            middle = velocity_ref[comp, s] - force_ref[at : at + 4, :] * factor
            last = middle - force_ref[48 + at : 48 + at + 4, :] * factor
            velocity_out_ref[comp, s] = last
            displacement_out_ref[comp, s] = displacement_ref[comp, s] + TIME_STEP * middle + TIME_STEP * last


def finish_kernel(velocity_ref, displacement_ref, mass_ref, middle_ref, in_low_ref, in_upper_ref, fields_ref,
                  velocity_out_ref, displacement_out_ref, stage_ref, force_ref):
    fields_ref[...] = sum_slots(middle_ref, in_low_ref, in_upper_ref)
    stage_ref[...] = join_edge(in_low_ref)
    interleave(stage_ref, force_ref)
    factor = TIME_STEP / mass_ref[0]
    for comp in range(3):
        change = force_ref[5 * comp : 5 * comp + 4, :] * factor
        velocity_out_ref[comp, 0] = velocity_ref[comp, 0] - change
        displacement_out_ref[comp, 0] = displacement_ref[comp, 0] - TIME_STEP * change


def fetch(sources, targets, sems):
    copies = [pltpu.make_async_copy(a, b, sems.at[i]) for i, (a, b) in enumerate(zip(sources, targets))]
    for copy in copies:
        copy.start()
    return copies


def pack_kernel(velocity_hbm, mass_hbm, send_a_ref, send_b_ref, send_c_ref, velocity_ref, mass_ref, sems):
    for copy in fetch((velocity_hbm, mass_hbm), (velocity_ref, mass_ref), sems):
        copy.wait()
    for comp in range(4):
        for s in range(4):
            own = mass_ref[s] if comp == 3 else velocity_ref[comp, s]
            if s == 0:
                send_a_ref[comp] = own
                send_c_ref[comp] = own[:1]
            send_b_ref[comp, s : s + 1, :] = own[:1]


def shape(*dims, dtype=F32):
    return jax.ShapeDtypeStruct(dims, dtype)


LATTICE = (3, ROWS, LINE)
FACE = (15, LINE)


def zone_scratch():
    return [
        pltpu.VMEM((15 * ROWS, 3 * ZONE_COUNT), BF16),
        pltpu.VMEM((3 * POINTS, 3 * ZONE_COUNT), BF16),
        pltpu.VMEM((3 * POINTS, 3 * ZONE_COUNT), BF16),
        pltpu.VMEM((POINTS, 2 * ZONE_COUNT), BF16),
        pltpu.VMEM((POINTS, 2 * ZONE_COUNT), BF16),
    ]


def whole(*dims):
    return pl.BlockSpec(dims, lambda i: (0,) * len(dims))


def cost(microseconds):
    return pl.CostEstimate(flops=int(microseconds * 1e9), bytes_accessed=int(microseconds * 3e6), transcendentals=0)


LIMIT = pltpu.CompilerParams(vmem_limit_bytes=40 * 1024 * 1024)
FAR = pl.BlockSpec(memory_space=pltpu.HBM)
ANYWHERE = pl.BlockSpec(memory_space=pl.ANY)
EDGE_BLOCK = pl.BlockSpec((16, SENT), lambda i: (CAPACITY // 16, 0))


def remap_call(step, blocks, rows, fields, modes, matrix, source, target):
    return pl.pallas_call(
        lambda *refs: remap_kernel(step, blocks, *refs),
        grid=(1,),
        in_specs=[whole(ZONE_COUNT, WIDTH), whole(2 * MODES, ZONE_COUNT), whole(STEPS, SLOTS), whole(STEPS, SLOTS)]
        + [pl.BlockSpec((1, CAPACITY, MODES, MODES), lambda i, block=block: (0, block, 0, 0)) for block in blocks],
        out_specs=[whole(CAPACITY, SENT)] * len(blocks),
        out_shape=[shape(count, SENT, dtype=BF16) for count in rows],
        scratch_shapes=[pltpu.VMEM((CAPACITY * len(blocks) * MODES, 128), F32)] * 2,
        compiler_params=LIMIT,
        cost_estimate=cost(0.7),
        name="remap_step",
    )(fields, modes, source, target, *[matrix] * len(blocks))


def far(*arrays):
    return [pltpu.with_memory_space_constraint(array, pltpu.HBM) for array in arrays]


def fold_call(source_row, block, edge, *faces):
    return pl.pallas_call(
        lambda *refs: fold_kernel(source_row, *refs),
        grid=(1,),
        in_specs=[ANYWHERE] + [whole(*FACE)] * (1 + len(faces)),
        out_specs=EDGE_BLOCK,
        out_shape=shape(FOLDED, SENT, dtype=BF16),
        input_output_aliases={0: 0},
        scratch_shapes=[pltpu.VMEM((16, LINE), F32)],
        compiler_params=LIMIT,
        cost_estimate=cost(0.5),
        name="fold_edges",
    )(block, edge, *near(*faces))


def near(*arrays):
    return [pltpu.with_memory_space_constraint(array, pltpu.VMEM) for array in arrays]


def body(fields, velocity, displacement, node_mass, remap_matrix, remap_source, remap_target):
    tables = basis_tables()
    lines = ("gx", "gy")
    send_a, send_b, send_c = pl.pallas_call(
        pack_kernel,
        in_specs=[FAR] * 2,
        out_shape=[shape(4, 4, LINE), shape(4, 4, LINE), shape(4, 1, LINE)],
        scratch_shapes=[
            pltpu.VMEM((3, 4, 4, LINE), F32),
            pltpu.VMEM((4, 4, LINE), F32),
            pltpu.SemaphoreType.DMA((2,)),
        ],
        compiler_params=LIMIT,
        cost_estimate=cost(1),
        name="pack_halo",
    )(*far(velocity, node_mass))
    size_a = lax.axis_size(lines)
    size_b = lax.axis_size("gz")
    corner = [
        (((i + 1) % size_a) * size_b + (j + 1) % size_b, i * size_b + j)
        for i in range(size_a)
        for j in range(size_b)
    ]
    halo_a = from_behind(send_a, lines, -1)
    halo_b = from_behind(send_b, "gz", -1)
    halo_c = lax.ppermute(send_c, ("gx", "gy", "gz"), corner)
    lattice = shape(*LATTICE)
    face = shape(*FACE)
    modes_shape = shape(2 * MODES, ZONE_COUNT, dtype=BF16)
    folded = shape(FOLDED, SENT, dtype=BF16)
    state, partial, up, edge_up, down, edge_down, modes = pl.pallas_call(
        zone_first_kernel,
        in_specs=[pl.BlockSpec(memory_space=pltpu.VMEM)] * 5 + [FAR] * 5,
        out_shape=[shape(4, ROWS, LINE), lattice, face, face, face, face, modes_shape],
        scratch_shapes=[pltpu.VMEM((4 * ROWS, LINE), F32)]
        + [pltpu.VMEM(array.shape, array.dtype) for array in (fields,) + tables]
        + [pltpu.SemaphoreType.DMA((5,))]
        + zone_scratch(),
        compiler_params=LIMIT,
        cost_estimate=cost(7),
        name="zone_first",
    )(velocity, node_mass, *near(halo_a, halo_b, halo_c), *far(fields, *tables))
    from_low = from_behind(up, "gz", 1)
    from_up = from_behind(down, "gz", -1)
    index = (remap_source, remap_target)
    matrix = remap_matrix[0:1]
    matrix_late = jnp.transpose(remap_matrix[1], (1, 2, 0))
    (upper,) = remap_call(0, (2,), (FOLDED,), fields, modes, matrix, *index)
    upper = fold_call(4, upper, edge_up, from_low, from_up)
    fields, modes, upper = lax.optimization_barrier((fields, modes, upper))
    in_low = from_behind(upper, lines, 1)
    (low,) = remap_call(0, (0,), (FOLDED,), fields, modes, matrix, *index)
    low = fold_call(0, low, edge_down, from_low, from_up)
    fields, modes, low, matrix_late = lax.optimization_barrier((fields, modes, low, matrix_late))
    in_upper = from_behind(low, lines, -1)
    (middle,) = remap_call(0, (1,), (CAPACITY,), fields, modes, matrix, *index)
    fields, first, partial, up, edge_up, modes = pl.pallas_call(
        zone_second_kernel,
        out_shape=[shape(ZONE_COUNT, WIDTH, dtype=BF16), lattice, lattice, face, face, modes_shape],
        scratch_shapes=[pltpu.VMEM((16, LINE), F32)] + zone_scratch(),
        compiler_params=LIMIT,
        cost_estimate=cost(7),
        name="zone_second",
    )(state, partial, *near(from_low, from_up), middle, *near(in_low, in_upper, *tables))
    from_low = from_behind(up, "gz", 1)
    matrix_late = with_layout_constraint(matrix_late, Layout(major_to_minor=(0, 1, 2)))
    matrix = jnp.transpose(matrix_late, (2, 0, 1))[None]
    (low,) = remap_call(1, (0,), (CAPACITY,), fields, modes, matrix, *index)
    fields, modes, low = lax.optimization_barrier((fields, modes, low))
    in_upper = from_behind(low, lines, -1)
    (upper,) = remap_call(1, (2,), (FOLDED,), fields, modes, matrix, *index)
    upper = fold_call(4, upper, edge_up, from_low)
    fields, modes, upper = lax.optimization_barrier((fields, modes, upper))
    in_low = from_behind(upper, lines, 1)
    (middle,) = remap_call(1, (1,), (CAPACITY,), fields, modes, matrix, *index)
    nodal = shape(*velocity.shape)
    velocity_part, displacement_part = pl.pallas_call(
        update_kernel,
        out_shape=[nodal, nodal],
        scratch_shapes=[pltpu.VMEM((96, LINE), F32)] * 2,
        compiler_params=LIMIT,
        cost_estimate=cost(2.5),
        name="update_nodes",
    )(velocity, displacement, node_mass, first, partial, *near(from_low))
    bottom = whole(3, 1, 4, LINE)
    fields_out, velocity_out, displacement_out = pl.pallas_call(
        finish_kernel,
        grid=(1,),
        in_specs=[
            bottom,
            bottom,
            whole(1, 4, LINE),
            whole(CAPACITY, SENT),
            whole(FOLDED, SENT),
            whole(CAPACITY, SENT),
        ],
        out_specs=[whole(ZONE_COUNT, WIDTH), bottom, bottom],
        out_shape=[shape(ZONE_COUNT, WIDTH, dtype=BF16), nodal, nodal],
        input_output_aliases={0: 1, 1: 2},
        scratch_shapes=[pltpu.VMEM((16, LINE), F32)] * 2,
        compiler_params=LIMIT,
        cost_estimate=cost(3),
        name="finish_step",
    )(velocity_part, displacement_part, node_mass, middle, *near(in_low, in_upper))
    return (fields_out, velocity_out, displacement_out)


def solution(mesh):
    in_specs = (
        P(("gx", "gy", "gz"), None),
        P(None, ("gx", "gy"), "gz", None),
        P(None, ("gx", "gy"), "gz", None),
        P(("gx", "gy"), "gz", None),
        P(None, ("gx", "gy", "gz"), None, None),
        P(None, ("gx", "gy", "gz")),
        P(None, ("gx", "gy", "gz")),
    )
    out_specs = (
        P(("gx", "gy", "gz"), None),
        P(None, ("gx", "gy"), "gz", None),
        P(None, ("gx", "gy"), "gz", None),
    )
    return jax.shard_map(body, mesh=mesh, in_specs=in_specs, out_specs=out_specs, check_vma=False)
```

```python
import math

import jax
import jax.numpy as jnp
import numpy as np
from jax import lax
from jax.experimental import pallas as pl
from jax.experimental.pallas import tpu as pltpu
from jax.sharding import PartitionSpec as P

NODES = 125
POINTS = 512
MODES = 64
FIELDS = 32
STEPS = 2


TIME_STEP = 0.3
GAMMA_LESS = 0.4
VISCOSITY = 0.3
F32 = jnp.float32
BF16 = jnp.bfloat16
ZONE_COUNT = 256
ROWS = 32
LINE = 1024
CAPACITY = 32
SLOTS = 96
WIDTH = MODES * FIELDS
SENT = WIDTH + 128
FOLDED = CAPACITY + 16


def from_behind(shard, axis, by):
    size = lax.axis_size(axis)
    return lax.ppermute(shard, axis, [(i, (i + by) % size) for i in range(size)])


def gauss_rule(order):
    if order == 8:
        half_points = [
            0.1834346424956498,
            0.525532409916329,
            0.7966664774136267,
            0.9602898564975363,
        ]
        half_weights = [
            0.362683783378362,
            0.3137066458778873,
            0.2223810344533745,
            0.1012285362903763,
        ]
    else:
        half_points = [0.3399810435848563, 0.8611363115940526]
        half_weights = [0.6521451548625461, 0.3478548451374538]
    points = np.array([-value for value in half_points[::-1]] + half_points)
    weights = np.array(half_weights[::-1] + half_weights)
    return (points, weights)


def lagrange_tables(nodes, points):
    values = np.ones((points.shape[0], nodes.shape[0]))
    slopes = np.zeros((points.shape[0], nodes.shape[0]))
    for column in range(nodes.shape[0]):
        for other in range(nodes.shape[0]):
            if other != column:
                values[:, column] *= (points - nodes[other]) / (nodes[column] - nodes[other])
        for other in range(nodes.shape[0]):
            if other != column:
                product = np.ones(points.shape) / (nodes[column] - nodes[other])
                for third in range(nodes.shape[0]):
                    if third != column and third != other:
                        product = product * (points - nodes[third]) / (nodes[column] - nodes[third])
                slopes[:, column] += product
    return (values, slopes)


def kron_three(first, second, third):
    return np.kron(np.kron(first, second), third)


def split_table(table):
    high = table.astype(jnp.bfloat16)
    low = (table - high.astype(np.float32)).astype(jnp.bfloat16)
    return (high, low)


def node_columns(table):
    grid = table.reshape(-1, 5, 25 // 5, 5).transpose(0, 3, 1, 2).reshape(-1, 5, 25)
    return np.pad(grid, ((0, 0), (0, 0), (0, ROWS - 25))).reshape(-1, 5 * ROWS)


def basis_tables():
    gauss_points, gauss_weights = gauss_rule(8)
    points = (gauss_points + 1.0) / 2.0
    weights = gauss_weights / 2.0
    root = math.sqrt(3.0 / 7.0)
    lobatto = (np.array([-1.0, -root, 0.0, root, 1.0]) + 1.0) / 2.0
    four_points, four_weights = gauss_rule(4)
    legendre_nodes = (four_points + 1.0) / 2.0
    node_values, node_slopes = lagrange_tables(lobatto, points)
    mode_values, unused_slopes = lagrange_tables(legendre_nodes, points)
    gradient_table = np.concatenate(
        [
            kron_three(node_slopes, node_values, node_values),
            kron_three(node_values, node_slopes, node_values),
            kron_three(node_values, node_values, node_slopes),
        ],
        0,
    )
    interpolate = kron_three(mode_values, mode_values, mode_values)
    weight_table = kron_three(weights, weights, weights)
    mass_diagonal = four_weights / 2.0
    project_line = mode_values.T * weights[None, :] / mass_diagonal[:, None]
    projection = kron_three(project_line, project_line, project_line)
    gradient_table = gradient_table.astype(np.float32)
    weighted_table = gradient_table * np.tile(weight_table.astype(np.float32), 3)[:, None]
    grad_hi, grad_lo = split_table(node_columns(gradient_table))
    force_hi, force_lo = split_table(node_columns(weighted_table).T)
    inter_hi, inter_lo = split_table(interpolate.astype(np.float32))
    proj_hi, proj_lo = split_table(projection.astype(np.float32))
    return (
        jnp.asarray(np.concatenate([grad_hi, grad_hi, grad_lo], 1)),
        jnp.asarray(np.concatenate([force_hi, force_lo], 0)),
        jnp.asarray(np.concatenate([inter_hi, inter_lo], 1)),
        jnp.asarray(np.concatenate([proj_hi, proj_lo], 0)),
    )


def split_two(values):
    high = values.astype(BF16)
    return (high, (values - high.astype(F32)).astype(BF16))


def split_three(values):
    high = values.astype(BF16)
    rest = values - high.astype(F32)
    middle = rest.astype(BF16)
    return (high, middle, (rest - middle.astype(F32)).astype(BF16))


def mm(left, right, dims=((1,), (0,))):
    return lax.dot_general(left, right, (dims, ((), ())), preferred_element_type=F32)


def iota(shape, axis):
    return lax.broadcasted_iota(jnp.int32, shape, axis)


def line_selector(to_zones):
    lattice = iota((512, 512), 0 if to_zones else 1)
    grouped = iota((512, 512), 1 if to_zones else 0)
    return jnp.where(4 * (grouped % 128) + grouped // 128 == lattice, 1.0, 0.0).astype(BF16)


def mode_columns():
    row = iota((2 * MODES, WIDTH), 0)
    column = iota((2 * MODES, WIDTH), 1)
    return jnp.where(FIELDS * (row % MODES) + row // MODES == column, 1.0, 0.0).astype(BF16)


def pick_modes(fields):
    return mm(mode_columns(), fields, ((1,), (1,)))


def zone_math(velocity_of, modes, grad_ref, force_ref, inter_ref, proj_ref, nodes_ref, high_ref, low_ref,
              rate_high_ref, rate_low_ref, lattice_ref, face_up_ref, edge_up_ref, face_down_ref, edge_down_ref, modes_ref):
    zones = ZONE_COUNT
    for comp in range(3):
        line = velocity_of(comp)
        lanes = slice(zones * comp, zones * (comp + 1))
        groups = [line[:, zones * u : zones * (u + 1)] for u in range(4)]
        groups.append(pltpu.roll(groups[0], zones - 1, 1))
        for u in range(5):
            high, low = split_two(groups[u])
            nodes_ref[ROWS * u : ROWS * (u + 1), lanes] = high
            nodes_ref[ROWS * (5 + u) : ROWS * (6 + u), lanes] = low
            nodes_ref[ROWS * (10 + u) : ROWS * (11 + u), lanes] = high
    both = jnp.concatenate([modes[:MODES], modes[MODES:]], 1)
    twice = jnp.concatenate([both, both], 0).astype(BF16)
    chunk = 128
    for part in range(POINTS // chunk):
        rows = slice(chunk * part, chunk * (part + 1))
        nodes = nodes_ref[...]
        grads = []
        for first in range(3):
            start = POINTS * first + chunk * part
            flat = mm(grad_ref[start : start + chunk, :], nodes)
            grads.append([flat[:, zones * c : zones * (c + 1)] for c in range(3)])
        points = mm(inter_ref[rows, :], twice)
        rho = points[:, :zones]
        energy = points[:, zones:]
        divergence = grads[0][0] + grads[1][1] + grads[2][2]
        pressure = GAMMA_LESS * energy
        viscous = 0.5 * VISCOSITY * rho
        heating = None
        for first in range(3):
            for second in range(first, 3):
                total = grads[first][second] + grads[second][first]
                entry = viscous * total
                if first == second:
                    entry = entry - pressure
                    work = entry * grads[first][first]
                else:
                    work = entry * total
                heating = work if heating is None else heating + work
                high, low = split_two(entry)
                for d, c in ((first, second), (second, first))[: 1 if first == second else 2]:
                    at = slice(POINTS * d + chunk * part, POINTS * d + chunk * (part + 1))
                    lanes = slice(zones * c, zones * (c + 1))
                    high_ref[at, lanes] = high
                    low_ref[at, lanes] = low
        for column, rate in ((0, -rho * divergence), (zones, heating - energy * divergence)):
            high, low = split_two(rate)
            rate_high_ref[rows, column : column + zones] = high
            rate_low_ref[rows, column : column + zones] = low
    nodal = 5 * ROWS
    main = mm(force_ref[...], high_ref[...])
    force = main[:nodal] + main[nodal:] + mm(force_ref[:nodal, :], low_ref[...])
    for comp in range(3):
        lanes = slice(zones * comp, zones * (comp + 1))
        for u in range(4):
            block = force[ROWS * u : ROWS * (u + 1), lanes]
            if u == 0:
                block = block + pltpu.roll(force[ROWS * 4 : ROWS * 5, lanes], 1, 1)
            lattice_ref[comp, :, zones * u : zones * (u + 1)] = block
    for comp in range(3):
        for s in range(5):
            face_up_ref[5 * comp + s, :] = lattice_ref[comp, 5 * s + 4, :]
            if face_down_ref is not None:
                face_down_ref[5 * comp + s, :] = lattice_ref[comp, 5 * s, :]
        edge_up_ref[5 * comp : 5 * comp + 5, :] = lattice_ref[comp, 20:25, :]
        if edge_down_ref is not None:
            edge_down_ref[5 * comp : 5 * comp + 5, :] = lattice_ref[comp, 0:5, :]
    main = mm(proj_ref[...], rate_high_ref[...])
    change = main[:MODES] + main[MODES:] + mm(proj_ref[:MODES, :], rate_low_ref[...])
    both = both + TIME_STEP * change
    modes_ref[:MODES, :] = both[:, :zones].astype(BF16)
    modes_ref[MODES:, :] = both[:, zones:].astype(BF16)


def zone_first_kernel(velocity_ref, mass_ref, halo_a_ref, halo_b_ref, halo_c_ref, fields_hbm, grad_hbm, force_hbm,
                      inter_hbm, proj_hbm, state_ref, lattice_ref, up_ref, edge_up_ref, down_ref, edge_down_ref, modes_ref,
                      native_ref, fields_ref, grad_ref, force_ref, inter_ref, proj_ref, sems, *scratch):
    copies = fetch(
        (fields_hbm, grad_hbm, force_hbm, inter_hbm, proj_hbm),
        (fields_ref, grad_ref, force_ref, inter_ref, proj_ref),
        sems,
    )
    for comp in range(4):
        base = ROWS * comp
        native_ref[base + 24 : base + 32, :] = jnp.full((8, LINE), 1.0 if comp == 3 else 0.0, F32)
        for s in range(4):
            own = mass_ref[s] if comp == 3 else velocity_ref[comp, s]
            native_ref[base + 5 * s : base + 5 * s + 4, :] = own
            native_ref[base + 5 * s + 4, :] = halo_b_ref[comp, s, :]
        native_ref[base + 20 : base + 24, :] = halo_a_ref[comp]
        native_ref[base + 24, :] = halo_c_ref[comp, 0, :]
    selector = line_selector(True)
    count = 4 * ROWS
    for half in range(2):
        pieces = jnp.concatenate(split_three(native_ref[:, 512 * half : 512 * (half + 1)]), 0)
        moved = mm(pieces, selector)
        moved = moved[:count] + moved[count : 2 * count] + moved[2 * count :]
        for comp in range(4):
            for u in range(4):
                lanes = slice(256 * u + 128 * half, 256 * u + 128 * (half + 1))
                state_ref[comp, :, lanes] = moved[ROWS * comp : ROWS * (comp + 1), 128 * u : 128 * (u + 1)]
    copies[0].wait()
    modes = pick_modes(fields_ref[...])
    for copy in copies[1:]:
        copy.wait()
    zone_math(lambda comp: state_ref[comp], modes, grad_ref, force_ref, inter_ref, proj_ref, *scratch,
              lattice_ref, up_ref, edge_up_ref, down_ref, edge_down_ref, modes_ref)


def add_faces(total_ref, low_ref, upper_ref):
    for comp in range(3):
        for s in range(5):
            at = 5 * comp + s
            total_ref[comp, 5 * s, :] = total_ref[comp, 5 * s, :] + low_ref[at, :]
            if upper_ref is not None:
                total_ref[comp, 5 * s + 4, :] = total_ref[comp, 5 * s + 4, :] + upper_ref[at, :]


def join_edge(block_ref):
    pair = block_ref[CAPACITY:FOLDED, :WIDTH].astype(F32)
    return pair[:, :LINE] + pair[:, LINE:]


def zone_second_kernel(state_ref, first_ref, low_ref, upper_ref, middle_ref, in_low_ref, in_upper_ref, grad_ref,
                       force_ref, inter_ref, proj_ref, fields_ref, total_ref, lattice_ref, up_ref, edge_up_ref,
                       modes_ref, edge_ref, *scratch):
    fields = sum_slots(middle_ref, in_low_ref, in_upper_ref)
    fields_ref[...] = fields
    total_ref[...] = first_ref[...]
    add_faces(total_ref, low_ref, upper_ref)
    for row, block_ref in ((0, in_low_ref), (20, in_upper_ref)):
        edge_ref[...] = join_edge(block_ref)
        for comp in range(3):
            at = slice(5 * comp, 5 * comp + 5)
            total_ref[comp, row : row + 5, :] = total_ref[comp, row : row + 5, :] + edge_ref[at, :]
    factor = TIME_STEP / state_ref[3]
    modes = pick_modes(fields)
    zone_math(lambda comp: state_ref[comp] - total_ref[comp] * factor, modes, grad_ref, force_ref, inter_ref,
              proj_ref, *scratch, lattice_ref, up_ref, edge_up_ref, None, None, modes_ref)


def sum_slots(*block_refs):
    incoming = jnp.concatenate([ref[:CAPACITY, :] for ref in block_refs], 0)
    codes = incoming[:, WIDTH:].astype(F32)
    label = iota((SLOTS, 128), 1).astype(F32)
    chosen = [jnp.where(codes == label + 128.0 * half, 1.0, 0.0).astype(BF16) for half in range(ZONE_COUNT // 128)]
    selector = jnp.concatenate(chosen, 1)
    return mm(selector, incoming[:, :WIDTH], ((0,), (0,))).astype(BF16)


def remap_kernel(step, blocks, fields_ref, modes_ref, source_ref, target_ref, *refs):
    number = len(blocks)
    matrix_refs, outs = refs[:number], refs[number : 2 * number]
    picked_ref, result_ref = refs[2 * number :]
    slots = CAPACITY * number

    def slots_of(ref):
        pieces = [ref[step : step + 1, CAPACITY * block : CAPACITY * (block + 1)] for block in blocks]
        return pieces[0] if number == 1 else jnp.concatenate(pieces, 1)

    zone = iota((ZONE_COUNT, slots), 0)
    chosen = jnp.where(zone == slots_of(source_ref), 1.0, 0.0).astype(BF16)
    picked = mm(chosen, fields_ref[...], ((0,), (0,)))
    new = mm(chosen, modes_ref[...].T, ((0,), (0,))).astype(BF16)
    new = mm(new, mode_columns())
    lane = iota((slots, 128), 1)
    group = lane // FIELDS
    renewed = lane % FIELDS < 2
    for g in range(WIDTH // 128):
        lanes = slice(128 * g, 128 * (g + 1))
        piece = jnp.where(renewed, new[:, lanes], picked[:, lanes])
        for r in range(4):
            picked_ref[pl.ds(4 * g + r, slots, stride=MODES), :] = jnp.where(group == r, piece, 0.0)
    for place, matrix_ref in enumerate(matrix_refs):

        def multiply(trip, carry):
            for inner in range(16):
                slot = 16 * trip + inner
                at = pl.ds(pl.multiple_of(MODES * (CAPACITY * place + slot), MODES), MODES)
                result_ref[at, :] = mm(matrix_ref[0, slot], picked_ref[at, :].astype(BF16))
            return carry

        lax.fori_loop(0, CAPACITY // 16, multiply, 0)
    for g in range(WIDTH // 128):
        rows = [result_ref[pl.ds(4 * g + r, slots, stride=MODES), :] for r in range(4)]
        total = None
        for shift in range(4):
            mixed = rows[3]
            for r in range(3):
                mixed = jnp.where(group == (r + shift) % 4, rows[r], mixed)
            if shift:
                mixed = pltpu.roll(mixed, 128 - FIELDS * shift, 1)
            total = mixed if total is None else total + mixed
        total = total.astype(BF16)
        for place in range(number):
            outs[place][:, 128 * g : 128 * (g + 1)] = total[CAPACITY * place : CAPACITY * (place + 1)]
    codes = jnp.broadcast_to(slots_of(target_ref).astype(F32), (8, slots))
    codes = jnp.where(iota((8, slots), 0) == 0, codes, 0.0).astype(BF16)
    codes = mm(codes, jnp.ones((8, 128), BF16), ((0,), (0,))).astype(BF16)
    for place in range(number):
        outs[place][:, WIDTH:] = codes[CAPACITY * place : CAPACITY * (place + 1)]


def fold_edge(edge_ref, source_row, low_ref, upper_ref, stage_ref, out_ref):
    stage_ref[15:16, :] = jnp.zeros((1, LINE), F32)
    stage_ref[0:15, :] = edge_ref[...]
    for comp in range(3):
        at = 5 * comp
        stage_ref[at, :] = stage_ref[at, :] + low_ref[at + source_row, :]
        if upper_ref is not None:
            stage_ref[at + 4, :] = stage_ref[at + 4, :] + upper_ref[at + source_row, :]
    high, low = split_two(stage_ref[...])
    out_ref[:, :LINE] = high
    out_ref[:, LINE:WIDTH] = low
    out_ref[:, WIDTH:] = jnp.zeros((16, 128), BF16)


def fold_kernel(source_row, block_any, edge_ref, *refs):
    upper_ref = refs[1] if len(refs) == 4 else None
    fold_edge(edge_ref, source_row, refs[0], upper_ref, refs[-1], refs[-2])


def interleave(stage_ref, force_ref):
    count = stage_ref.shape[0]
    selector = line_selector(False)
    for half in range(2):
        grouped = jnp.concatenate(
            [stage_ref[:, 256 * u + 128 * half : 256 * u + 128 * (half + 1)] for u in range(4)], 1
        )
        moved = mm(jnp.concatenate(split_two(grouped), 0), selector)
        force_ref[:, 512 * half : 512 * (half + 1)] = moved[:count] + moved[count:]


def update_kernel(velocity_ref, displacement_ref, mass_ref, first_ref, second_ref, low_ref, velocity_out_ref,
                  displacement_out_ref, stage_ref, force_ref):
    for comp in range(3):
        for s in range(4):
            at = 16 * comp + 4 * s
            stage_ref[at : at + 4, :] = first_ref[comp, 5 * s : 5 * s + 4, :]
            stage_ref[48 + at : 48 + at + 4, :] = second_ref[comp, 5 * s : 5 * s + 4, :]
            stage_ref[48 + at, :] = stage_ref[48 + at, :] + low_ref[5 * comp + s, :]
    interleave(stage_ref, force_ref)
    for s in range(4):
        factor = TIME_STEP / mass_ref[s]
        for comp in range(3):
            at = 16 * comp + 4 * s
            middle = velocity_ref[comp, s] - force_ref[at : at + 4, :] * factor
            last = middle - force_ref[48 + at : 48 + at + 4, :] * factor
            velocity_out_ref[comp, s] = last
            displacement_out_ref[comp, s] = displacement_ref[comp, s] + TIME_STEP * middle + TIME_STEP * last


def finish_kernel(velocity_ref, displacement_ref, mass_ref, middle_ref, in_low_ref, in_upper_ref, fields_ref,
                  velocity_out_ref, displacement_out_ref, stage_ref, force_ref):
    fields_ref[...] = sum_slots(middle_ref, in_low_ref, in_upper_ref)
    stage_ref[...] = join_edge(in_low_ref)
    interleave(stage_ref, force_ref)
    factor = TIME_STEP / mass_ref[0]
    for comp in range(3):
        change = force_ref[5 * comp : 5 * comp + 4, :] * factor
        velocity_out_ref[comp, 0] = velocity_ref[comp, 0] - change
        displacement_out_ref[comp, 0] = displacement_ref[comp, 0] - TIME_STEP * change


def fetch(sources, targets, sems):
    copies = [pltpu.make_async_copy(a, b, sems.at[i]) for i, (a, b) in enumerate(zip(sources, targets))]
    for copy in copies:
        copy.start()
    return copies


def pack_kernel(velocity_hbm, mass_hbm, send_a_ref, send_b_ref, send_c_ref, velocity_ref, mass_ref, sems):
    for copy in fetch((velocity_hbm, mass_hbm), (velocity_ref, mass_ref), sems):
        copy.wait()
    for comp in range(4):
        for s in range(4):
            own = mass_ref[s] if comp == 3 else velocity_ref[comp, s]
            if s == 0:
                send_a_ref[comp] = own
                send_c_ref[comp] = own[:1]
            send_b_ref[comp, s : s + 1, :] = own[:1]


def shape(*dims, dtype=F32):
    return jax.ShapeDtypeStruct(dims, dtype)


LATTICE = (3, ROWS, LINE)
FACE = (15, LINE)


def zone_scratch():
    return [
        pltpu.VMEM((15 * ROWS, 3 * ZONE_COUNT), BF16),
        pltpu.VMEM((3 * POINTS, 3 * ZONE_COUNT), BF16),
        pltpu.VMEM((3 * POINTS, 3 * ZONE_COUNT), BF16),
        pltpu.VMEM((POINTS, 2 * ZONE_COUNT), BF16),
        pltpu.VMEM((POINTS, 2 * ZONE_COUNT), BF16),
    ]


def whole(*dims):
    return pl.BlockSpec(dims, lambda i: (0,) * len(dims))


def cost(microseconds):
    return pl.CostEstimate(flops=int(microseconds * 1e9), bytes_accessed=int(microseconds * 3e6), transcendentals=0)


LIMIT = pltpu.CompilerParams(vmem_limit_bytes=40 * 1024 * 1024)
FAR = pl.BlockSpec(memory_space=pltpu.HBM)
ANYWHERE = pl.BlockSpec(memory_space=pl.ANY)
EDGE_BLOCK = pl.BlockSpec((16, SENT), lambda i: (CAPACITY // 16, 0))


def remap_call(step, blocks, rows, fields, modes, matrix, source, target):
    return pl.pallas_call(
        lambda *refs: remap_kernel(step, blocks, *refs),
        grid=(1,),
        in_specs=[whole(ZONE_COUNT, WIDTH), whole(2 * MODES, ZONE_COUNT), whole(STEPS, SLOTS), whole(STEPS, SLOTS)]
        + [pl.BlockSpec((1, CAPACITY, MODES, MODES), lambda i, block=block: (0, block, 0, 0)) for block in blocks],
        out_specs=[whole(CAPACITY, SENT)] * len(blocks),
        out_shape=[shape(count, SENT, dtype=BF16) for count in rows],
        scratch_shapes=[pltpu.VMEM((CAPACITY * len(blocks) * MODES, 128), F32)] * 2,
        compiler_params=LIMIT,
        cost_estimate=cost(0.7),
        name="remap_step",
    )(fields, modes, source, target, *[matrix] * len(blocks))


def far(*arrays):
    return [pltpu.with_memory_space_constraint(array, pltpu.HBM) for array in arrays]


def fold_call(source_row, block, edge, *faces):
    return pl.pallas_call(
        lambda *refs: fold_kernel(source_row, *refs),
        grid=(1,),
        in_specs=[ANYWHERE] + [whole(*FACE)] * (1 + len(faces)),
        out_specs=EDGE_BLOCK,
        out_shape=shape(FOLDED, SENT, dtype=BF16),
        input_output_aliases={0: 0},
        scratch_shapes=[pltpu.VMEM((16, LINE), F32)],
        compiler_params=LIMIT,
        cost_estimate=cost(0.5),
        name="fold_edges",
    )(block, edge, *near(*faces))


def near(*arrays):
    return [pltpu.with_memory_space_constraint(array, pltpu.VMEM) for array in arrays]


def body(fields, velocity, displacement, node_mass, remap_matrix, remap_source, remap_target):
    tables = basis_tables()
    lines = ("gx", "gy")
    send_a, send_b, send_c = pl.pallas_call(
        pack_kernel,
        in_specs=[FAR] * 2,
        out_shape=[shape(4, 4, LINE), shape(4, 4, LINE), shape(4, 1, LINE)],
        scratch_shapes=[
            pltpu.VMEM((3, 4, 4, LINE), F32),
            pltpu.VMEM((4, 4, LINE), F32),
            pltpu.SemaphoreType.DMA((2,)),
        ],
        compiler_params=LIMIT,
        cost_estimate=cost(1),
        name="pack_halo",
    )(*far(velocity, node_mass))
    size_a = lax.axis_size(lines)
    size_b = lax.axis_size("gz")
    corner = [
        (((i + 1) % size_a) * size_b + (j + 1) % size_b, i * size_b + j)
        for i in range(size_a)
        for j in range(size_b)
    ]
    halo_a = from_behind(send_a, lines, -1)
    halo_b = from_behind(send_b, "gz", -1)
    halo_c = lax.ppermute(send_c, ("gx", "gy", "gz"), corner)
    lattice = shape(*LATTICE)
    face = shape(*FACE)
    modes_shape = shape(2 * MODES, ZONE_COUNT, dtype=BF16)
    folded = shape(FOLDED, SENT, dtype=BF16)
    state, partial, up, edge_up, down, edge_down, modes = pl.pallas_call(
        zone_first_kernel,
        in_specs=[pl.BlockSpec(memory_space=pltpu.VMEM)] * 5 + [FAR] * 5,
        out_shape=[shape(4, ROWS, LINE), lattice, face, face, face, face, modes_shape],
        scratch_shapes=[pltpu.VMEM((4 * ROWS, LINE), F32)]
        + [pltpu.VMEM(array.shape, array.dtype) for array in (fields,) + tables]
        + [pltpu.SemaphoreType.DMA((5,))]
        + zone_scratch(),
        compiler_params=LIMIT,
        cost_estimate=cost(7),
        name="zone_first",
    )(velocity, node_mass, *near(halo_a, halo_b, halo_c), *far(fields, *tables))
    from_low = from_behind(up, "gz", 1)
    from_up = from_behind(down, "gz", -1)
    index = (remap_source, remap_target)
    matrix = remap_matrix[0:1]
    matrix_late = remap_matrix[1:2]
    low, upper = remap_call(0, (0, 2), (FOLDED, FOLDED), fields, modes, matrix, *index)
    upper = fold_call(4, upper, edge_up, from_low, from_up)
    low = fold_call(0, low, edge_down, from_low, from_up)
    in_low = from_behind(upper, lines, 1)
    fields, modes, low, matrix_late = lax.optimization_barrier((fields, modes, low, matrix_late))
    in_upper = from_behind(low, lines, -1)
    (middle,) = remap_call(0, (1,), (CAPACITY,), fields, modes, matrix, *index)
    fields, first, partial, up, edge_up, modes = pl.pallas_call(
        zone_second_kernel,
        out_shape=[shape(ZONE_COUNT, WIDTH, dtype=BF16), lattice, lattice, face, face, modes_shape],
        scratch_shapes=[pltpu.VMEM((16, LINE), F32)] + zone_scratch(),
        compiler_params=LIMIT,
        cost_estimate=cost(7),
        name="zone_second",
    )(state, partial, *near(from_low, from_up), middle, *near(in_low, in_upper, *tables))
    from_low = from_behind(up, "gz", 1)
    matrix = matrix_late
    (low,) = remap_call(1, (0,), (CAPACITY,), fields, modes, matrix, *index)
    fields, modes, low = lax.optimization_barrier((fields, modes, low))
    in_upper = from_behind(low, lines, -1)
    (upper,) = remap_call(1, (2,), (FOLDED,), fields, modes, matrix, *index)
    upper = fold_call(4, upper, edge_up, from_low)
    fields, modes, upper = lax.optimization_barrier((fields, modes, upper))
    in_low = from_behind(upper, lines, 1)
    (middle,) = remap_call(1, (1,), (CAPACITY,), fields, modes, matrix, *index)
    nodal = shape(*velocity.shape)
    velocity_part, displacement_part = pl.pallas_call(
        update_kernel,
        out_shape=[nodal, nodal],
        scratch_shapes=[pltpu.VMEM((96, LINE), F32)] * 2,
        compiler_params=LIMIT,
        cost_estimate=cost(2.5),
        name="update_nodes",
    )(velocity, displacement, node_mass, first, partial, *near(from_low))
    bottom = whole(3, 1, 4, LINE)
    fields_out, velocity_out, displacement_out = pl.pallas_call(
        finish_kernel,
        grid=(1,),
        in_specs=[
            bottom,
            bottom,
            whole(1, 4, LINE),
            whole(CAPACITY, SENT),
            whole(FOLDED, SENT),
            whole(CAPACITY, SENT),
        ],
        out_specs=[whole(ZONE_COUNT, WIDTH), bottom, bottom],
        out_shape=[shape(ZONE_COUNT, WIDTH, dtype=BF16), nodal, nodal],
        input_output_aliases={0: 1, 1: 2},
        scratch_shapes=[pltpu.VMEM((16, LINE), F32)] * 2,
        compiler_params=LIMIT,
        cost_estimate=cost(3),
        name="finish_step",
    )(velocity_part, displacement_part, node_mass, middle, *near(in_low, in_upper))
    return (fields_out, velocity_out, displacement_out)


def solution(mesh):
    in_specs = (
        P(("gx", "gy", "gz"), None),
        P(None, ("gx", "gy"), "gz", None),
        P(None, ("gx", "gy"), "gz", None),
        P(("gx", "gy"), "gz", None),
        P(None, ("gx", "gy", "gz"), None, None),
        P(None, ("gx", "gy", "gz")),
        P(None, ("gx", "gy", "gz")),
    )
    out_specs = (
        P(("gx", "gy", "gz"), None),
        P(None, ("gx", "gy"), "gz", None),
        P(None, ("gx", "gy"), "gz", None),
    )
    return jax.shard_map(body, mesh=mesh, in_specs=in_specs, out_specs=out_specs, check_vma=False)
```
